512 devices in a mesh: seq: 128 (over y, x, z_hi, core), head: 4 (over z_lo).
Axes of the slice: x: 4, y: 4, z: 16 (z_hi: 4, z_lo: 4; z = z_hi * 4 + z_lo), core: 2. Of those that a mesh axis runs over, the one named last changes fastest.
Arguments:
- tokens: int32 [16384], P('seq'), may hold values from 0 to 11
- residual_in: bfloat16 [16384, 2048], P('seq'), may hold values from -5 to 5
- pairing: int32 [2048], replicated, may hold values from 0 to 2047, as said below
- embedding: bfloat16 [12, 2048], replicated, may hold values from -5 to 5
- x_weight: bfloat16 [2048, 2048], P(None, 'head'), may hold values from -0.125 to 0.125
- bc_weight: bfloat16 [2048, 256], replicated, may hold values from -0.03125 to 0.03125
- dt_weight: bfloat16 [2048, 32], P(None, 'head'), may hold values from -0.125 to 0.125
- dt_bias: float32 [32], P('head'), may hold values from -8 to -1
- decay_rate: float32 [32], P('head'), may hold values from 0 to 1
- skip_gain: float32 [32], P('head'), may hold values from 0.5 to 1.5
- cotangent: bfloat16 [16384, 2048], P('seq', 'head'), may hold values from -6 to 6
Outputs:
- input_grad: float32 [2048, 16384], P('head', 'seq')
- saliency: float32 [16384], P('seq')
The draws below stay inside these ranges and needn't reach their ends.
Inputs may be any that keep to these rules, and one draw needn't show every extreme that they name: pairing[pairing[d]] = d and pairing[d] != d.
All inputs are finite; a program needn't handle non-finite values.
Results may differ from the reference program's by a relative error of at most 0.0056.
Values sent between devices are 32-bit elements; how exact they have to be, the bound alone decides.
A program may use at most 64 MiB of HBM per device.

```python
import math
import jax
import jax.numpy as jnp
from jax import lax

D = 2048
HEADS = 32
HEADDIM = 64
STATE = 128
VOCAB = 12
GROUP = 128
INNER = 2048
TOKENS = 16384


def rate_helper(key):
    folded = jax.random.fold_in(key, 11)
    order = jax.random.permutation(jax.random.fold_in(folded, 1), HEADS)
    slow_heads = order < HEADS // 2
    spread_draw = jax.random.uniform(jax.random.fold_in(folded, 2), (HEADS,), jnp.float32)
    slow_log = jnp.log(0.05 / TOKENS) + spread_draw * jnp.log(10.0)
    fast_low = jnp.log(4.0 / TOKENS)
    fast_log = fast_low + spread_draw * (jnp.log(1.0 / 30.0) - fast_low)
    return jnp.where(slow_heads, slow_log, fast_log)


def draw_decay_rate(key, part):
    log_eps = rate_helper(key)
    noise = jax.random.uniform(jax.random.fold_in(key, 12), (HEADS,), jnp.float32, -0.3, 0.3)
    return jnp.exp(0.5 * log_eps + noise)


def draw_dt_bias(key, part):
    log_eps = rate_helper(key)
    return jnp.log(jnp.expm1(jnp.exp(0.5 * log_eps)))


def draw_pairing(key, part):
    order = jax.random.permutation(jax.random.fold_in(key, 21), D).astype(jnp.int32)
    partner = order.reshape(-1, 2)[:, ::-1].reshape(-1)
    return jnp.zeros((D,), jnp.int32).at[order].set(partner)


def plant(array, own_key, least, largest):
    longest = array.shape.index(max(array.shape))
    spots = []
    for shift in (0, 1):
        where = [jax.random.randint(jax.random.fold_in(own_key, axis), (), 0, length) for axis, length in enumerate(array.shape)]
        where[longest] = (where[longest] + shift) % array.shape[longest]
        spots.append(tuple(where))
    return array.at[spots[0]].set(least).at[spots[1]].set(largest)


def shard_levels(own_key, shape, split, smallest, high):
    def one(axis_at, shards_of):
        steps = jax.random.uniform(jax.random.fold_in(jax.random.fold_in(own_key, 6), axis_at), (shards_of,), jnp.float32, smallest / len(split), high / len(split))
        return jnp.repeat(jnp.exp(steps), shape[axis_at] // shards_of).reshape((-1,) + (1,) * (len(shape) - axis_at - 1))

    loudness = one(*split[0])
    for cut in split[1:]:
        loudness = loudness * one(*cut)
    return loudness


def bell_draw(key, shape, width, bound, shards=(), dtype=jnp.bfloat16):
    gain = shard_levels(key, shape, shards, -0.22, 0.18) if shards else 1.0
    array = jax.random.normal(key, shape, jnp.float32) * width * gain
    return jnp.minimum(jnp.maximum(array, -bound), bound).astype(dtype)


def setup_inputs(seed: int = 0) -> dict:
    splits = jax.random.split(jax.random.key(seed), 12)
    tokens = plant(jax.random.randint(splits[0], (TOKENS,), 0, VOCAB), jax.random.fold_in(splits[0], 1), 0, VOCAB - 1).astype(jnp.int32)
    residual_in = bell_draw(splits[1], (TOKENS, D), 0.7, 5.0, ((0, 128),))
    pairing = draw_pairing(jax.random.fold_in(splits[11], 71), 0)
    embedding = bell_draw(splits[3], (VOCAB, D), 0.7, 5.0)
    x_weight = bell_draw(splits[4], (D, INNER), D ** -0.5, 0.125, ((1, 4),))
    bc_weight = bell_draw(splits[5], (D, 2 * STATE), (D * STATE // 8) ** -0.5, 0.03125)
    dt_weight = bell_draw(splits[6], (D, HEADS), D ** -0.5, 0.125, ((1, 4),))
    dt_bias = draw_dt_bias(jax.random.fold_in(splits[11], 71), 0)
    decay_rate = draw_decay_rate(jax.random.fold_in(splits[11], 71), 0)
    skip_gain = jnp.clip(0.5 + 1.0 * jax.random.uniform(splits[9], (HEADS,), jnp.float32) ** shard_levels(splits[9], (HEADS,), ((0, 4),), -0.2, 0.2), 0.5, 1.5)
    cotangent = bell_draw(splits[10], (TOKENS, INNER), 1.0, 6.0, ((0, 128), (1, 4)))
    return dict(tokens=tokens, residual_in=residual_in, pairing=pairing, embedding=embedding, x_weight=x_weight, bc_weight=bc_weight, dt_weight=dt_weight, dt_bias=dt_bias, decay_rate=decay_rate, skip_gain=skip_gain, cotangent=cotangent)


highest = lax.Precision.HIGHEST

def strides(pre, dt_bias, decay_rate):
    stride = jax.nn.softplus(pre + dt_bias[None, :])
    return (stride, -decay_rate[None, :] * stride)

def group_scan(inputs, writer, reader, pre, dt_bias, decay_rate, skip_gain, start):
    stride, log_decay = strides(pre, dt_bias, decay_rate)
    length = inputs.shape[0]
    blocks = length // GROUP
    heads = inputs.shape[1]
    headdim = inputs.shape[2]
    state_dim = writer.shape[1]
    causal = (jnp.arange(GROUP)[:, None] >= jnp.arange(GROUP)[None, :])[:, :, None]

    def advance(state, pieces):
        in_block, write_block, read_block, stride_block, decay_block = pieces
        running = jnp.cumsum(decay_block, axis=0)
        from_state = jnp.exp(running)[:, :, None] * jnp.einsum('hpn,qn->qhp', state, read_block, precision=highest)
        scores = jnp.einsum('qn,sn->qs', read_block, write_block, precision=highest)
        spread = running[:, None, :] - running[None, :, :]
        weights = jnp.exp(jnp.where(causal, spread, -jnp.inf)) * scores[:, :, None] * stride_block[None, :, :]
        within = jnp.einsum('qsh,shp->qhp', weights, in_block, precision=highest)
        result = from_state + within + skip_gain[None, :, None] * in_block
        last_sum = running[-1]
        carry_weight = jnp.exp(last_sum[None, :] - running) * stride_block
        state = jnp.exp(last_sum)[:, None, None] * state + jnp.einsum('sh,shp,sn->hpn', carry_weight, in_block, write_block, precision=highest)
        return (state, result)
    pieces = (inputs.reshape(blocks, GROUP, heads, headdim), writer.reshape(blocks, GROUP, state_dim), reader.reshape(blocks, GROUP, state_dim), stride.reshape(blocks, GROUP, heads), log_decay.reshape(blocks, GROUP, heads))
    final, outputs = lax.scan(jax.checkpoint(advance), start, pieces)
    return (outputs.reshape(length, heads, headdim), final)

def reference(tokens, residual_in, pairing, embedding, x_weight, bc_weight, dt_weight, dt_bias, decay_rate, skip_gain, cotangent):
    layer_in = (embedding.astype(jnp.float32)[tokens] + residual_in.astype(jnp.float32)).astype(jnp.bfloat16)
    upstream = cotangent.astype(jnp.float32).reshape(TOKENS, HEADS, HEADDIM)
    anchor = jnp.zeros((HEADS, HEADDIM, STATE), jnp.float32)

    def branch(source, upper):
        inputs = jnp.dot(source, x_weight, preferred_element_type=jnp.float32).reshape(TOKENS, HEADS, HEADDIM)
        mixed = jnp.dot(source, bc_weight, preferred_element_type=jnp.float32)
        pre = jnp.dot(source, dt_weight, preferred_element_type=jnp.float32)

        def mixer(inputs, writer, reader, pre):
            return group_scan(inputs, writer, reader, pre, dt_bias, decay_rate, skip_gain, anchor)[0]
        outputs, pull = jax.vjp(mixer, inputs, mixed[:, :STATE], mixed[:, STATE:], pre)
        d_inputs, d_writer, d_reader, d_pre = pull(upper)
        d_inputs16 = d_inputs.reshape(TOKENS, INNER).astype(jnp.bfloat16)
        d_pre16 = d_pre.astype(jnp.bfloat16)
        d_mixed = jnp.concatenate([d_writer, d_reader], axis=1)
        back = jnp.dot(d_inputs16, x_weight.T, preferred_element_type=jnp.float32)
        back = back + jnp.dot(d_pre16, dt_weight.T, preferred_element_type=jnp.float32)
        back = back + jnp.dot(d_mixed, bc_weight.astype(jnp.float32).T, precision=highest)
        return back
    forward_back = branch(layer_in, upstream)
    paired = jnp.take(layer_in, pairing, axis=1)
    reverse_back = jnp.flip(branch(jnp.flip(paired, 0), jnp.flip(upstream, 0)), 0)
    layer_grad = forward_back + jnp.take(reverse_back, pairing, axis=1)
    saliency = lax.optimization_barrier(jnp.sum(layer_grad * layer_in.astype(jnp.float32), axis=1)) / math.sqrt(D)
    return (layer_grad.T, saliency)
```

```python
import functools
import math

import jax
import jax.numpy as jnp
from jax import lax
from jax.experimental import pallas as pl
from jax.experimental.pallas import tpu as pltpu
from jax.sharding import PartitionSpec as P

L = 128
H = 8
HP = 512
N = 128
WIDTH = 2048
TILE = 256
F32 = jnp.float32
BF16 = jnp.bfloat16
NEG = -1e30
MESH = pl.DeviceIdType.MESH

NN = (((1,), (0,)), ((), ()))
NT = (((1,), (1,)), ((), ()))
TN = (((0,), (0,)), ((), ()))


def exact(a, b, dims=NN):
    return lax.dot_general(a, b, dims, precision=lax.Precision.HIGHEST, preferred_element_type=F32)


def fast(a, b, dims=NN):
    return lax.dot_general(a.astype(BF16), b.astype(BF16), dims, preferred_element_type=F32)


def iota(shape, axis):
    return lax.broadcasted_iota(jnp.int32, shape, axis)


def head_rows():
    return (iota((H, HP), 1) // 64 == iota((H, HP), 0)).astype(F32)


def reach(branch):
    row, col = iota((L, L), 0), iota((L, L), 1)
    return col <= row if branch == 0 else col >= row


def rates(pre, bias, rate):
    z = pre + bias
    stride = jnp.maximum(z, 0.0) + jnp.log1p(jnp.exp(-jnp.abs(z)))
    return z, stride, -rate * stride


def embed(tokens_row, embedding, residual):
    vocab = embedding.shape[0]
    hot = (iota((vocab, L), 0) == tokens_row).astype(F32).T.astype(BF16)
    return (
        jnp.dot(hot, embedding, preferred_element_type=F32) + residual.astype(F32)
    ).astype(BF16)


def summaries(branch, x, mixed, pre, bias, rate, upstream):
    _, stride, log_decay = rates(pre, bias, rate)
    run = exact(reach(branch).astype(F32), log_decay)
    total = jnp.sum(log_decay, axis=0, keepdims=True)
    spread = head_rows()
    carry = exact(jnp.exp(total - run) * stride, spread)
    grown = exact(jnp.exp(run), spread)
    end = fast((x * carry).T, mixed[:, :N])
    direct = fast((upstream * grown).T, mixed[:, N:])
    return jnp.exp(total), end, direct


def backward(branch, x, mixed, pre, bias, rate, skip, upstream, entry, later):
    writer, reader = mixed[:, :N], mixed[:, N:]
    z, stride, log_decay = rates(pre, bias, rate)
    mask = reach(branch)
    mask_t = reach(1 - branch)
    run = exact(mask.astype(F32), log_decay)
    run_t = run.T
    total = jnp.sum(log_decay, axis=0, keepdims=True)
    spread = head_rows()
    stride_e = exact(stride, spread)
    decay_e = exact(jnp.exp(total - run), spread)
    grown = upstream * exact(jnp.exp(run), spread)
    carried = x * stride_e * decay_e
    low_half = iota((L, 2 * 64), 1) < 64
    scores_t = fast(writer, reader, NT)
    ups = upstream.astype(F32)
    volume = jnp.zeros((L, L), F32)
    rows = []
    pieces = []
    for pair in range(H // 2):
        lanes = slice(128 * pair, 128 * pair + 128)
        x_pair, u_pair = x[:, lanes], ups[:, lanes]
        kernels, uppers = [], []
        for half in range(2):
            h = 2 * pair + half
            mine = low_half if half == 0 else jnp.logical_not(low_half)
            u_half = jnp.where(mine, u_pair, 0.0)
            fade = jnp.exp(jnp.where(mask_t, run_t[h : h + 1, :] - run[:, h : h + 1], NEG))
            cross = fast(x_pair, u_half, NT)
            weight = fade * cross * stride[:, h : h + 1]
            volume = volume + weight
            rows.append(jnp.sum(weight * scores_t, axis=0, keepdims=True))
            kernels.append((fade * scores_t).astype(BF16))
            uppers.append(u_half.astype(BF16))
        pieces.append(fast(jnp.concatenate(kernels, axis=1), jnp.concatenate(uppers, axis=0)))
    pushed = fast(writer, later, NT)
    inner = jnp.concatenate(pieces, axis=1) + decay_e * pushed
    d_inputs = exact(skip, spread) * ups + stride_e * inner
    d_writer = fast(volume, reader) + fast(carried, later)
    d_reader = fast(volume.T, writer) + fast(grown, entry)
    pulled = fast(reader, entry, NT)
    spread_t = spread.T
    per_write = exact(x * inner, spread_t)
    tail = exact(carried * pushed, spread_t)
    per_read = jnp.concatenate(rows, axis=0).T + exact(grown * pulled, spread_t)
    dots = exact(spread, entry * later)
    overlap = exact(jnp.ones((8, L), F32), dots, NT)[0:1]
    d_total = jnp.exp(total) * overlap + jnp.sum(tail, axis=0, keepdims=True)
    d_run = per_read - stride * per_write
    d_log = exact(mask_t.astype(F32), d_run) + d_total
    d_stride = per_write - rate * d_log
    d_pre = d_stride / (1.0 + jnp.exp(-z))
    return d_inputs, d_pre, d_writer, d_reader


def project(source, x_weight, bc_weight, dt_weight):
    dot = functools.partial(jnp.dot, preferred_element_type=F32)
    return dot(source, x_weight), dot(source, bc_weight), dot(source, dt_weight)


def permutation(pairing_row, first, count, axis):
    shape = (WIDTH, count) if axis == 1 else (count, WIDTH)
    return (iota(shape, 0) + (0 if axis == 1 else first) == pairing_row).astype(F32).astype(BF16)


def padded_rows(factor, first):
    wide = jnp.broadcast_to(factor, (H, H))
    own = jnp.where(iota((H, H), 0) + first == iota((H, H), 1), wide, 0.0)
    return jnp.broadcast_to(jnp.sum(own, axis=1, keepdims=True), (H, N))


def front_kernel(
    tokens, residual, pairing, embedding, x_weight, bc_weight, dt_weight, bias, rate, cotangent,
    x_out, mixed_out, pre_out, layer_t, sums, source,
):
    layer = embed(tokens[...], embedding[...], residual[...])
    layer_t[...] = layer.astype(F32).T.astype(BF16)
    for block in range(WIDTH // TILE):
        cols = slice(TILE * block, TILE * block + TILE)
        hot = permutation(pairing[:, cols], 0, TILE, 1)
        source[:, cols] = jnp.dot(layer, hot, preferred_element_type=F32).astype(BF16)
    upstream = cotangent[...].astype(F32)
    for branch in range(2):
        read = layer if branch == 0 else source[...]
        x, mixed, pre = project(read, x_weight[...], bc_weight[...], dt_weight[...])
        x_out[branch] = x
        mixed_out[branch] = mixed
        pre_out[branch] = pre
        factor, end, direct = summaries(branch, x, mixed, pre, bias[...], rate[...], upstream)
        up, down = (end, direct) if branch == 0 else (direct, end)
        for way, value in ((0, up), (1, down)):
            for part in range(2):
                piece = 2 * branch + part
                sums[way, piece, 0:256, :] = value[256 * part : 256 * part + 256]
                sums[way, piece, 256:264, :] = padded_rows(factor, 4 * part)


def scaled(factors, values):
    return jnp.concatenate(
        [factors[i : i + 1, :] * values[64 * i : 64 * i + 64, :] for i in range(4)], axis=0
    )


def after(later, earlier):
    values = scaled(later[256:264], earlier[0:256]) + later[0:256]
    return jnp.concatenate([values, later[256:264] * earlier[256:264]], axis=0)


def scan_kernel(sums, out, partner, chip, z_in, z_pre, x_in, y_in, e_line, e_out, e_in, far, far_in, send, recv):
    seq, head = lax.axis_index("seq"), lax.axis_index("head")
    core = lax.rem(seq, 2)
    z = lax.rem(seq // 2, 4)
    x = lax.rem(seq // 8, 4)
    y = seq // 32

    def device(yy, xx, zz, cc):
        return (((yy * 4 + xx) * 4 + zz) * 2 + cc, head)

    def other(value, step):
        return lax.rem(value + step, 4)

    mate = device(y, x, z, 1 - core)
    z_peer = [device(y, x, other(z, d), core) for d in (1, 2, 3)]
    x_peer = [device(y, other(x, d), z, core) for d in (1, 2, 3)]
    y_peer = [device(other(y, d), x, z, core) for d in (1, 2, 3)]
    barrier = pltpu.get_barrier_semaphore()
    for peer in [mate] + z_peer + x_peer + y_peer:
        pl.semaphore_signal(barrier, inc=1, device_id=peer, device_id_type=MESH)
    pl.semaphore_wait(barrier, 10)

    def push(source, target, slot, peer):
        copy = pltpu.make_async_remote_copy(
            src_ref=source, dst_ref=target, send_sem=send.at[slot], recv_sem=recv.at[slot],
            device_id=peer, device_id_type=MESH,
        )
        copy.start()
        return copy

    first = [push(sums.at[1 - core, q], partner.at[q], q, mate) for q in range(4)]
    for q in range(4):
        first[q].wait_recv()
        chip[q] = after(partner[q], sums[core, q])
    z_copies = [push(chip.at[other(z, d)], z_in.at[z], 3 + d, z_peer[d - 1]) for d in (1, 2, 3)]
    z_in[z] = chip[z]
    for copy in z_copies:
        copy.wait_recv()

    def place(j):
        return jnp.where(core == 0, j, 3 - j)

    line = z_in[place(0)]
    for j in range(1, 4):
        z_pre[place(j)] = line
        line = after(z_in[place(j)], line)
    x_in[x] = line
    x_copies = [push(x_in.at[x], x_in.at[x], 6 + d, x_peer[d - 1]) for d in (1, 2, 3)]
    for copy in x_copies:
        copy.wait_recv()
    blank = jnp.concatenate([jnp.zeros((256, N), F32), jnp.ones((8, N), F32)], axis=0)

    def before(held, mine):
        total, prefix = blank, blank
        for j in range(4):
            spot = place(j)
            prefix = jnp.where(spot == mine, total, prefix)
            total = after(held[spot], total)
        return prefix, total

    x_prefix, x_total = before(x_in, x)
    y_in[y] = x_total
    y_copies = [push(y_in.at[y], y_in.at[y], 9 + d, y_peer[d - 1]) for d in (1, 2, 3)]
    for copy in y_copies:
        copy.wait_recv()
    y_prefix, _ = before(y_in, y)
    e_line[...] = after(x_prefix, y_prefix)
    e_out[place(0)] = e_line[0:256, :]
    for j in range(1, 4):
        held = z_pre[place(j)]
        e_out[place(j)] = scaled(held[256:264], e_line[0:256, :]) + held[0:256]
    e_copies = [push(e_out.at[other(z, d)], e_in.at[z], 12 + d, z_peer[d - 1]) for d in (1, 2, 3)]
    e_in[z] = e_out[z]
    for copy in e_copies:
        copy.wait_recv()
    for q in range(4):
        value = sums[core, q]
        far[q] = scaled(value[256:264], e_in[q]) + value[0:256]
        out[core, q] = e_in[q]
    last = [push(far.at[q], far_in.at[q], 16 + q, mate) for q in range(4)]
    for q in range(4):
        last[q].wait_recv()
        out[1 - core, q] = far_in[q]
    for copy in first + z_copies + x_copies + y_copies + e_copies + last:
        copy.wait_send()


def grad_kernel(x, mixed, pre, bias, rate, skip, cotangent, states, d_x, d_mixed, d_pre):
    upstream = cotangent[...].astype(F32)
    for branch in range(2):
        way = (0, 1) if branch == 0 else (1, 0)

        def whole(direction):
            return jnp.concatenate([states[direction, 2 * branch], states[direction, 2 * branch + 1]], axis=0)

        entry, later = whole(way[0]), whole(way[1])
        g_x, g_pre, g_writer, g_reader = backward(
            branch, x[branch], mixed[branch], pre[branch], bias[...], rate[...], skip[...],
            upstream, entry, later,
        )
        d_x[branch] = g_x.astype(BF16)
        d_pre[branch] = g_pre.astype(BF16)
        for column, value in ((0, g_writer), (N, g_reader)):
            high = value.astype(BF16)
            d_mixed[branch, 0, :, column : column + N] = high
            d_mixed[branch, 1, :, column : column + N] = (value - high.astype(F32)).astype(BF16)


def paired_kernel(pairing, x_weight, bc_weight, dt_weight, x_out, bc_out, dt_out):
    for block in range(WIDTH // TILE):
        rows = slice(TILE * block, TILE * block + TILE)
        hot = permutation(pairing[...], TILE * block, TILE, 0)
        for weight, target in ((x_weight, x_out), (bc_weight, bc_out), (dt_weight, dt_out)):
            target[rows, :] = jnp.dot(hot, weight[...], preferred_element_type=F32).astype(BF16)


def back_kernel(
    x_weight, bc_weight, dt_weight, x_paired, bc_paired, dt_paired, d_x, d_mixed, d_pre, layer_t,
    grad, saliency, part, got, sal_part, sal_got, send, recv,
):
    seq, head = lax.axis_index("seq"), lax.axis_index("head")

    def peer(step):
        return (seq, lax.rem(head + step, 4))

    barrier = pltpu.get_barrier_semaphore()
    for step in (1, 2, 3):
        pl.semaphore_signal(barrier, inc=1, device_id=peer(step), device_id_type=MESH)
    pl.semaphore_wait(barrier, 3)
    rows_here = WIDTH // 4

    def push(source, target, slot, device):
        copy = pltpu.make_async_remote_copy(
            src_ref=source, dst_ref=target, send_sem=send.at[slot], recv_sem=recv.at[slot],
            device_id=device, device_id_type=MESH,
        )
        copy.start()
        return copy

    def chunk(owner):
        rows = pl.ds(pl.multiple_of(owner * rows_here, rows_here), rows_here)
        total = jnp.zeros((rows_here, L), F32)
        for branch, weights in (
            (0, (x_weight, bc_weight, dt_weight)),
            (1, (x_paired, bc_paired, dt_paired)),
        ):
            total = total + lax.dot_general(weights[0][rows, :], d_x[branch], NT, preferred_element_type=F32)
            for term in range(2):
                total = total + lax.dot_general(
                    weights[1][rows, :], d_mixed[branch, term], NT, preferred_element_type=F32
                )
            total = total + lax.dot_general(weights[2][rows, :], d_pre[branch], NT, preferred_element_type=F32)
        weighed = jnp.sum(total * layer_t[rows, :].astype(F32), axis=0, keepdims=True)
        return total, weighed

    copies = []
    weighed = jnp.zeros((1, L), F32)
    for step in (1, 2, 3):
        owner = lax.rem(head + step, 4)
        total, share = chunk(owner)
        weighed = weighed + share
        part[step - 1] = total
        copies.append(push(part.at[step - 1], got.at[step - 1], step - 1, peer(step)))
    total, share = chunk(head)
    weighed = weighed + share
    sal_part[...] = jnp.broadcast_to(weighed, (8, L))
    sal_got[head] = sal_part[...]
    for step in (1, 2, 3):
        copies.append(push(sal_part, sal_got.at[head], 2 + step, peer(step)))
    for copy in copies:
        copy.wait_recv()
    grad[...] = ((total + got[0]) + got[1]) + got[2]
    saliency[...] = (
        ((sal_got[0, 0:1] + sal_got[1, 0:1]) + sal_got[2, 0:1]) + sal_got[3, 0:1]
    ) / math.sqrt(WIDTH)
    for copy in copies:
        copy.wait_send()


VM = pl.BlockSpec(memory_space=pltpu.VMEM)


def call(kernel, outs, count, scratch=(), comm=None):
    return pl.pallas_call(
        kernel,
        out_shape=[jax.ShapeDtypeStruct(shape, dtype) for shape, dtype in outs],
        in_specs=[VM] * count,
        out_specs=[VM] * len(outs),
        scratch_shapes=list(scratch),
        compiler_params=pltpu.CompilerParams(
            collective_id=comm, has_side_effects=comm is not None, vmem_limit_bytes=60 << 20
        ),
    )


def shards(
    tokens, residual_in, pairing, embedding, x_weight, bc_weight, dt_weight, dt_bias, decay_rate,
    skip_gain, cotangent,
):
    tokens_row, pairing_row = tokens.reshape(1, L), pairing.reshape(1, WIDTH)
    bias, rate, skip = (value.reshape(1, H) for value in (dt_bias, decay_rate, skip_gain))
    x, mixed, pre, layer_t, sums = call(
        front_kernel,
        [
            ((2, L, HP), F32), ((2, L, 2 * N), F32), ((2, L, H), F32), ((WIDTH, L), BF16),
            ((2, 4, 264, N), F32),
        ],
        10,
        [pltpu.VMEM((L, WIDTH), BF16)],
    )(tokens_row, residual_in, pairing_row, embedding, x_weight, bc_weight, dt_weight, bias, rate, cotangent)
    block = pltpu.VMEM((4, 264, N), F32)
    plain = pltpu.VMEM((4, 256, N), F32)
    (states,) = call(
        scan_kernel,
        [((2, 4, 256, N), F32)],
        1,
        [
            block, block, block, block, block, block, pltpu.VMEM((264, N), F32), plain, plain,
            plain, plain, pltpu.SemaphoreType.DMA((20,)), pltpu.SemaphoreType.DMA((20,)),
        ],
        comm=0,
    )(sums)
    x_paired, bc_paired, dt_paired = call(
        paired_kernel, [((WIDTH, HP), BF16), ((WIDTH, 2 * N), BF16), ((WIDTH, H), BF16)], 4
    )(pairing_row, x_weight, bc_weight, dt_weight)
    d_x, d_mixed, d_pre = call(
        grad_kernel,
        [((2, L, HP), BF16), ((2, 2, L, 2 * N), BF16), ((2, L, H), BF16)],
        8,
    )(x, mixed, pre, bias, rate, skip, cotangent, states)
    grad, saliency = call(
        back_kernel,
        [((WIDTH // 4, L), F32), ((1, L), F32)],
        10,
        [
            pltpu.VMEM((3, WIDTH // 4, L), F32), pltpu.VMEM((3, WIDTH // 4, L), F32),
            pltpu.VMEM((8, L), F32), pltpu.VMEM((4, 8, L), F32),
            pltpu.SemaphoreType.DMA((6,)), pltpu.SemaphoreType.DMA((6,)),
        ],
        comm=1,
    )(x_weight, bc_weight, dt_weight, x_paired, bc_paired, dt_paired, d_x, d_mixed, d_pre, layer_t)
    return grad, saliency.reshape(L)


def solution(mesh):
    return jax.shard_map(
        shards,
        mesh=mesh,
        in_specs=(
            P("seq"), P("seq", None), P(), P(), P(None, "head"), P(), P(None, "head"), P("head"),
            P("head"), P("head"), P("seq", "head"),
        ),
        out_specs=(P("head", "seq"), P("seq")),
        check_vma=False,
    )
```

```python
import functools
import math

import jax
import jax.numpy as jnp
from jax import lax
from jax.experimental import pallas as pl
from jax.experimental.pallas import tpu as pltpu
from jax.sharding import PartitionSpec as P

L = 128
H = 8
HP = 512
N = 128
WIDTH = 2048
TILE = 256
F32 = jnp.float32
BF16 = jnp.bfloat16
NEG = -1e30
MESH = pl.DeviceIdType.MESH

NN = (((1,), (0,)), ((), ()))
NT = (((1,), (1,)), ((), ()))
TN = (((0,), (0,)), ((), ()))


def fast(a, b, dims=NN):
    return lax.dot_general(a.astype(BF16), b.astype(BF16), dims, preferred_element_type=F32)


def parts(a, terms=3):
    held = []
    for _ in range(terms):
        held.append(a.astype(BF16))
        a = a - held[-1].astype(F32)
    return held


def split(a, b, dims=NN, right=False):
    if right:
        a, b = a.astype(BF16), parts(b)
        return sum(lax.dot_general(a, p, dims, preferred_element_type=F32) for p in b)
    b = b.astype(BF16)
    return sum(lax.dot_general(p, b, dims, preferred_element_type=F32) for p in parts(a))


def split_right(a, b):
    return split(a, b, NN, True)


def iota(shape, axis):
    return lax.broadcasted_iota(jnp.int32, shape, axis)


def head_rows():
    return (iota((H, HP), 1) // 64 == iota((H, HP), 0)).astype(F32)


def reach(branch):
    row, col = iota((L, L), 0), iota((L, L), 1)
    return col <= row if branch == 0 else col >= row


def rates(pre, bias, rate):
    z = pre + bias
    stride = jnp.maximum(z, 0.0) + jnp.log1p(jnp.exp(-jnp.abs(z)))
    return z, stride, -rate * stride


def embed(tokens_row, embedding, residual):
    vocab = embedding.shape[0]
    hot = (iota((vocab, L), 0) == tokens_row).astype(F32).T.astype(BF16)
    return (
        jnp.dot(hot, embedding, preferred_element_type=F32) + residual.astype(F32)
    ).astype(BF16)


def summaries(branch, x, mixed, pre, bias, rate, upstream):
    _, stride, log_decay = rates(pre, bias, rate)
    run = split_right(reach(branch).astype(F32), log_decay)
    total = jnp.sum(log_decay, axis=0, keepdims=True)
    spread = head_rows()
    carried = x * split(jnp.exp(total - run) * stride, spread)
    grown = upstream * split(jnp.exp(run), spread)
    end = fast(carried.T, mixed[:, :N])
    direct = fast(grown.T, mixed[:, N:])
    return jnp.exp(total), end, direct, carried, grown


def local_grads(branch, x, mixed, pre, bias, rate, skip, ups):
    writer, reader = mixed[:, :N], mixed[:, N:]
    _, stride, log_decay = rates(pre, bias, rate)
    mask_t = reach(1 - branch)
    run = split_right(reach(branch).astype(F32), log_decay)
    run_t = run.T
    spread = head_rows()
    low_half = iota((L, 2 * 64), 1) < 64
    scores_t = fast(writer, reader, NT)
    volume = jnp.zeros((L, L), F32)
    rows = []
    pieces = []
    for pair in range(H // 2):
        lanes = slice(128 * pair, 128 * pair + 128)
        x_pair, u_pair = x[:, lanes], ups[:, lanes]
        kernels, uppers = [], []
        for half in range(2):
            h = 2 * pair + half
            mine = low_half if half == 0 else jnp.logical_not(low_half)
            u_half = jnp.where(mine, u_pair, 0.0)
            fade = jnp.exp(jnp.where(mask_t, run_t[h : h + 1, :] - run[:, h : h + 1], NEG))
            cross = fast(x_pair, u_half, NT)
            weight = fade * cross * stride[:, h : h + 1]
            volume = volume + weight
            rows.append(jnp.sum(weight * scores_t, axis=0, keepdims=True))
            kernels.append((fade * scores_t).astype(BF16))
            uppers.append(u_half.astype(BF16))
        pieces.append(fast(jnp.concatenate(kernels, axis=1), jnp.concatenate(uppers, axis=0)))
    inner = jnp.concatenate(pieces, axis=1)
    d_inputs = split(skip, spread) * ups + split(stride, spread) * inner
    per_write = split(x * inner, spread.T)
    per_read = jnp.concatenate(rows, axis=0).T
    return d_inputs, fast(volume, reader), fast(volume.T, writer), per_read, per_write


def full_grads(branch, x, mixed, pre, bias, rate, carried, grown, entry, later, local):
    d_inputs, d_writer, d_reader, per_read, per_write = local
    writer, reader = mixed[:, :N], mixed[:, N:]
    z, stride, log_decay = rates(pre, bias, rate)
    run = split_right(reach(branch).astype(F32), log_decay)
    total = jnp.sum(log_decay, axis=0, keepdims=True)
    spread = head_rows()
    spread_t = spread.T
    outer = split(jnp.exp(total - run), spread) * fast(writer, later, NT)
    d_inputs = d_inputs + split(stride, spread) * outer
    d_writer = d_writer + fast(carried, later)
    d_reader = d_reader + fast(grown, entry)
    written = split(x * outer, spread_t)
    per_write = per_write + written
    per_read = per_read + split(grown * fast(reader, entry, NT), spread_t)
    dots = split_right(spread, entry * later)
    overlap = split(jnp.ones((8, L), F32), dots, NT, True)[0:1]
    d_total = jnp.exp(total) * overlap + jnp.sum(stride * written, axis=0, keepdims=True)
    d_run = per_read - stride * per_write
    d_log = split_right(reach(1 - branch).astype(F32), d_run) + d_total
    d_stride = per_write - rate * d_log
    d_pre = d_stride / (1.0 + jnp.exp(-z))
    return d_inputs, d_pre, d_writer, d_reader


def project(source, x_weight, bc_weight, dt_rows):
    dot = functools.partial(jnp.dot, preferred_element_type=F32)
    pre = lax.dot_general(source, dt_rows, NT, preferred_element_type=F32)
    return dot(source, x_weight), dot(source, bc_weight), pre


def permutation(pairing_row, first, count, axis):
    shape = (WIDTH, count) if axis == 1 else (count, WIDTH)
    return (iota(shape, 0) + (0 if axis == 1 else first) == pairing_row).astype(F32).astype(BF16)


def padded_rows(factor, first):
    wide = jnp.broadcast_to(factor, (H, H))
    own = jnp.where(iota((H, H), 0) + first == iota((H, H), 1), wide, 0.0)
    return jnp.broadcast_to(jnp.sum(own, axis=1, keepdims=True), (H, N))


def front_kernel(
    tokens, residual, pairing, embedding, x_weight, bc_weight, dt_rows, bias, rate, cotangent,
    x_out, mixed_out, pre_out, carried_out, grown_out, layer_t, sums, factors, source,
):
    layer = embed(tokens[...], embedding[...], residual[...])
    layer_t[...] = layer.astype(F32).T.astype(BF16)
    for block in range(WIDTH // TILE):
        cols = slice(TILE * block, TILE * block + TILE)
        hot = permutation(pairing[:, cols], 0, TILE, 1)
        source[:, cols] = jnp.dot(layer, hot, preferred_element_type=F32).astype(BF16)
    upstream = cotangent[...].astype(F32)
    for branch in range(2):
        read = layer if branch == 0 else source[...]
        x, mixed, pre = project(read, x_weight[...], bc_weight[...], dt_rows[...])
        x_out[branch] = x
        mixed_out[branch] = mixed
        pre_out[branch] = pre
        factor, end, direct, carried, grown = summaries(
            branch, x, mixed, pre, bias[...], rate[...], upstream
        )
        carried_out[branch] = carried.astype(BF16)
        grown_out[branch] = grown
        up, down = (end, direct) if branch == 0 else (direct, end)
        for way, value in ((0, up), (1, down)):
            for h in range(H):
                sums[way, h % 4, 2 * branch + h // 4] = value[64 * h : 64 * h + 64]
        for part in range(2):
            factors[2 * branch + part] = padded_rows(factor, 4 * part)


def scan_kernel(
    sums, factors, pairing, x_weight, bc_weight, dt_rows, x, mixed, pre, bias, rate, skip, cotangent,
    out, x_out, bc_out, dt_out, g_x, g_mixed, g_read, g_write,
    mate_in, mate_fac, chip, z_in, z_pre, x_in, y_in, e_out, e_in, far, far_in, x_fac, z_fac, send, recv,
):
    seq, head = lax.axis_index("seq"), lax.axis_index("head")
    core = lax.rem(seq, 2)
    z = lax.rem(seq // 2, 4)
    xx = lax.rem(seq // 8, 4)
    yy = seq // 32

    def device(y_at, x_at, z_at, core_at):
        return (((y_at * 4 + x_at) * 4 + z_at) * 2 + core_at, head)

    def other(value, step):
        return lax.rem(value + step, 4)

    mate = device(yy, xx, z, 1 - core)
    z_peer = [device(yy, xx, other(z, d), core) for d in (1, 2, 3)]
    x_peer = [device(yy, other(xx, d), z, core) for d in (1, 2, 3)]
    y_peer = [device(other(yy, d), xx, z, core) for d in (1, 2, 3)]
    barrier = pltpu.get_barrier_semaphore()
    for peer in [mate] + z_peer + x_peer + y_peer:
        pl.semaphore_signal(barrier, inc=1, device_id=peer, device_id_type=MESH)
    pl.semaphore_wait(barrier, 10)
    started = []

    def push(source, target, slot, peer):
        copy = pltpu.make_async_remote_copy(
            src_ref=source, dst_ref=target, send_sem=send.at[slot], recv_sem=recv.at[slot],
            device_id=peer, device_id_type=MESH,
        )
        copy.start()
        started.append(copy)
        return copy

    def place(j):
        return jnp.where(core == 0, j, 3 - j)

    def size(k):
        return pl.ds(0, 72 if k == 0 else 64)

    mate_f = push(factors, mate_fac, 0, mate)
    mate_s = [push(sums.at[1 - core, k], mate_in.at[k], 1 + k, mate) for k in range(4)]
    mate_f.wait_recv()
    z_s, x_s, y_s, e_s, far_s = [], [], [], [], []
    for k in range(4):
        mate_s[k].wait_recv()
        for q in range(4):
            chip[k, q, 0:64, :] = (
                mate_fac[q, k : k + 1, :] * sums[core, k, q] + mate_in[k, q]
            )
            if k == 0:
                chip[k, q, 64:72, :] = mate_fac[q] * factors[q]
        z_s.append([
            push(chip.at[k, other(z, d), size(k)], z_in.at[k, z, size(k)], 4 + 3 * k + d, z_peer[d - 1])
            for d in (1, 2, 3)
        ])
        z_in[k, z] = chip[k, z]

    def z_step(k):
        for copy in z_s[k]:
            copy.wait_recv()
        first = place(0)
        line = z_in[k, first, 0:64, :]
        factor = z_in[0, first, 64:72, :]
        for j in range(1, 4):
            spot = place(j)
            z_pre[k, spot] = line
            if k == 0:
                z_fac[spot] = factor
                factor = factor * z_in[0, spot, 64:72, :]
            line = z_in[0, spot, 64 + k : 65 + k, :] * line + z_in[k, spot, 0:64, :]
        x_in[k, xx, 0:64, :] = line
        if k == 0:
            x_in[k, xx, 64:72, :] = factor
        x_s.append([
            push(x_in.at[k, xx, size(k)], x_in.at[k, xx, size(k)], 16 + 3 * k + d, x_peer[d - 1])
            for d in (1, 2, 3)
        ])

    def before(held, k, mine):
        total, prefix = jnp.zeros((64, N), F32), jnp.zeros((64, N), F32)
        for j in range(4):
            spot = place(j)
            prefix = jnp.where(spot == mine, total, prefix)
            total = held[0, spot, 64 + k : 65 + k, :] * total + held[k, spot, 0:64, :]
        return prefix, total

    x_prefix = [None] * 4

    def x_step(k):
        for copy in x_s[k]:
            copy.wait_recv()
        x_prefix[k], total = before(x_in, k, xx)
        y_in[k, yy, 0:64, :] = total
        if k == 0:
            factor, prefix = jnp.ones((8, N), F32), jnp.ones((8, N), F32)
            for j in range(4):
                spot = place(j)
                prefix = jnp.where(spot == xx, factor, prefix)
                factor = factor * x_in[0, spot, 64:72, :]
            x_fac[...] = prefix
            y_in[k, yy, 64:72, :] = factor
        y_s.append([
            push(y_in.at[k, yy, size(k)], y_in.at[k, yy, size(k)], 28 + 3 * k + d, y_peer[d - 1])
            for d in (1, 2, 3)
        ])

    def y_step(k):
        for copy in y_s[k]:
            copy.wait_recv()
        y_prefix, _ = before(y_in, k, yy)
        line = x_fac[k : k + 1, :] * y_prefix + x_prefix[k]
        e_out[k, place(0)] = line
        for j in range(1, 4):
            spot = place(j)
            e_out[k, spot] = z_fac[spot, k : k + 1, :] * line + z_pre[k, spot]
        e_s.append([
            push(e_out.at[k, other(z, d)], e_in.at[k, z], 40 + 3 * k + d, z_peer[d - 1])
            for d in (1, 2, 3)
        ])
        e_in[k, z] = e_out[k, z]

    z_step(0)
    z_step(1)
    x_step(0)
    y_step(0)
    z_step(2)
    x_step(1)
    y_step(1)
    z_step(3)
    x_step(2)
    y_step(2)
    x_step(3)
    y_step(3)

    ups = cotangent[...].astype(F32)
    for branch in range(2):
        d_in, d_w, d_r, per_read, per_write = local_grads(
            branch, x[branch], mixed[branch], pre[branch], bias[...], rate[...], skip[...], ups
        )
        g_x[branch] = d_in
        g_mixed[branch, :, 0:N] = d_w
        g_mixed[branch, :, N : 2 * N] = d_r
        g_read[branch] = per_read
        g_write[branch] = per_write
    for block in range(WIDTH // TILE):
        rows = slice(TILE * block, TILE * block + TILE)
        hot = permutation(pairing[...], TILE * block, TILE, 0)
        for weight, target in ((x_weight, x_out), (bc_weight, bc_out)):
            target[rows, :] = jnp.dot(hot, weight[...], preferred_element_type=F32).astype(BF16)
        dt_out[:, rows] = lax.dot_general(
            dt_rows[...], hot, NT, preferred_element_type=F32
        ).astype(BF16)

    for k in range(4):
        for copy in e_s[k]:
            copy.wait_recv()
        for q in range(4):
            far[k, q] = factors[q, k : k + 1, :] * e_in[k, q] + sums[core, k, q]
            out[core, k, q] = e_in[k, q]
        far_s.append(push(far.at[k], far_in.at[k], 53 + k, mate))
    for k in range(4):
        far_s[k].wait_recv()
        out[1 - core, k] = far_in[k]
    for copy in started:
        copy.wait_send()


def back_kernel(
    x_weight, bc_weight, dt_rows, x_paired, bc_paired, dt_paired, x, mixed, pre, bias, rate,
    carried, grown, states, g_x, g_mixed, g_read, g_write, layer_t,
    grad, saliency, part, got, d_x, d_mixed, d_pre, sal_part, sal_got, send, recv,
):
    seq, head = lax.axis_index("seq"), lax.axis_index("head")

    def peer(index):
        return (seq, index)

    barrier = pltpu.get_barrier_semaphore()
    for step in (1, 2, 3):
        pl.semaphore_signal(barrier, inc=1, device_id=peer(lax.rem(head + step, 4)), device_id_type=MESH)
    pl.semaphore_wait(barrier, 3)
    for branch in range(2):
        way = (0, 1) if branch == 0 else (1, 0)

        def whole(direction):
            return jnp.concatenate(
                [states[direction, h % 4, 2 * branch + h // 4] for h in range(H)], axis=0
            )

        local = (
            g_x[branch], g_mixed[branch, :, 0:N], g_mixed[branch, :, N : 2 * N], g_read[branch],
            g_write[branch],
        )
        full_x, full_pre, g_writer, g_reader = full_grads(
            branch, x[branch], mixed[branch], pre[branch], bias[...], rate[...], carried[branch],
            grown[branch], whole(way[0]), whole(way[1]), local,
        )
        d_x[branch] = full_x.astype(BF16)
        d_pre[branch] = full_pre.astype(BF16)
        for column, value in ((0, g_writer), (N, g_reader)):
            high = value.astype(BF16)
            d_mixed[branch, 0, :, column : column + N] = high
            d_mixed[branch, 1, :, column : column + N] = (value - high.astype(F32)).astype(BF16)
    rows_here = WIDTH // 4

    def push(source, target, sent, slot, device):
        copy = pltpu.make_async_remote_copy(
            src_ref=source, dst_ref=target, send_sem=send.at[sent], recv_sem=recv.at[slot],
            device_id=device, device_id_type=MESH,
        )
        copy.start()
        return copy

    def chunk(owner):
        first = pl.multiple_of(owner * rows_here, rows_here)
        rows = pl.ds(first, rows_here)
        total = jnp.zeros((rows_here, L), F32)
        for branch, weights in (
            (0, (x_weight, bc_weight, dt_rows)),
            (1, (x_paired, bc_paired, dt_paired)),
        ):
            total = total + lax.dot_general(weights[0][rows, :], d_x[branch], NT, preferred_element_type=F32)
            for term in range(2):
                total = total + lax.dot_general(
                    weights[1][rows, :], d_mixed[branch, term], NT, preferred_element_type=F32
                )
            dt_cols = weights[2][:, rows].astype(F32).T.astype(BF16)
            total = total + lax.dot_general(dt_cols, d_pre[branch], NT, preferred_element_type=F32)
        weighed = jnp.sum(total * layer_t[rows, :].astype(F32), axis=0, keepdims=True)
        return total, weighed

    edge = jnp.logical_or(head == 0, head == 3)
    near = jnp.where(head < 2, 1, 2)
    second = jnp.where(head == 0, 2, jnp.where(head == 1, 0, jnp.where(head == 2, 3, 1)))
    third = jnp.where(head == 0, 1, jnp.where(head == 1, 3, jnp.where(head == 2, 0, 2)))
    total, weighed = chunk(3 - head)
    part[0] = total
    to_first = jnp.where(edge, near, 3 - head)
    slot = jnp.where(edge, 0, 1)
    copies = [push(part.at[0], got.at[slot], 0, slot, peer(to_first))]
    total, share = chunk(second)
    weighed = weighed + share
    part[1] = total
    copies.append(push(part.at[1], got.at[2], 1, 2, peer(second)))
    total, share = chunk(third)
    weighed = weighed + share
    part[2] = total

    def arrived(index):
        pltpu.make_async_remote_copy(
            src_ref=part.at[0], dst_ref=got.at[index], send_sem=send.at[0], recv_sem=recv.at[index],
            device_id=peer(3 - head), device_id_type=MESH,
        ).wait_recv()

    @pl.when(jnp.logical_not(edge))
    def _():
        arrived(0)
        part[2] = part[2] + got[0]

    copies.append(push(part.at[2], got.at[3], 2, 3, peer(third)))
    total, share = chunk(head)
    weighed = weighed + share
    grad[...] = total
    sal_part[...] = jnp.broadcast_to(weighed, (8, L))
    sal_got[head] = sal_part[...]
    shares = [
        push(sal_part, sal_got.at[head], 2 + step, 3 + step, peer(lax.rem(head + step, 4)))
        for step in (1, 2, 3)
    ]
    for copy in shares:
        copy.wait_recv()
    saliency[...] = (
        ((sal_got[0, 0:1] + sal_got[1, 0:1]) + sal_got[2, 0:1]) + sal_got[3, 0:1]
    ) / math.sqrt(WIDTH)

    @pl.when(jnp.logical_not(edge))
    def _():
        arrived(1)
        grad[...] = grad[...] + got[1]

    arrived(2)
    grad[...] = grad[...] + got[2]
    arrived(3)
    grad[...] = grad[...] + got[3]
    for copy in copies + shares:
        copy.wait_send()


VM = pl.BlockSpec(memory_space=pltpu.VMEM)


def call(kernel, outs, count, scratch=(), comm=None):
    return pl.pallas_call(
        kernel,
        out_shape=[jax.ShapeDtypeStruct(shape, dtype) for shape, dtype in outs],
        in_specs=[VM] * count,
        out_specs=[VM] * len(outs),
        scratch_shapes=list(scratch),
        compiler_params=pltpu.CompilerParams(
            collective_id=comm, has_side_effects=comm is not None, vmem_limit_bytes=60 << 20
        ),
    )


def shards(
    tokens, residual_in, pairing, embedding, x_weight, bc_weight, dt_weight, dt_bias, decay_rate,
    skip_gain, cotangent,
):
    tokens_row, pairing_row = tokens.reshape(1, L), pairing.reshape(1, WIDTH)
    bias, rate, skip = (value.reshape(1, H) for value in (dt_bias, decay_rate, skip_gain))
    dt_rows = dt_weight.T
    x, mixed, pre, carried, grown, layer_t, sums, factors = call(
        front_kernel,
        [
            ((2, L, HP), F32), ((2, L, 2 * N), F32), ((2, L, H), F32), ((2, L, HP), BF16),
            ((2, L, HP), F32), ((WIDTH, L), BF16), ((2, 4, 4, 64, N), F32), ((4, 8, N), F32),
        ],
        10,
        [pltpu.VMEM((L, WIDTH), BF16)],
    )(tokens_row, residual_in, pairing_row, embedding, x_weight, bc_weight, dt_rows, bias, rate, cotangent)
    plain = pltpu.VMEM((4, 4, 64, N), F32)
    tall = pltpu.VMEM((4, 4, 72, N), F32)
    states, x_paired, bc_paired, dt_paired, g_x, g_mixed, g_read, g_write = call(
        scan_kernel,
        [
            ((2, 4, 4, 64, N), F32), ((WIDTH, HP), BF16), ((WIDTH, 2 * N), BF16), ((H, WIDTH), BF16),
            ((2, L, HP), F32), ((2, L, 2 * N), F32), ((2, L, H), F32), ((2, L, H), F32),
        ],
        13,
        [
            plain, pltpu.VMEM((4, 8, N), F32), tall, tall, plain, tall, tall, plain, plain, plain, plain,
            pltpu.VMEM((8, N), F32), pltpu.VMEM((4, 8, N), F32), pltpu.SemaphoreType.DMA((57,)),
            pltpu.SemaphoreType.DMA((57,)),
        ],
        comm=0,
    )(sums, factors, pairing_row, x_weight, bc_weight, dt_rows, x, mixed, pre, bias, rate, skip, cotangent)
    grad, saliency = call(
        back_kernel,
        [((WIDTH // 4, L), F32), ((1, L), F32)],
        19,
        [
            pltpu.VMEM((3, WIDTH // 4, L), F32), pltpu.VMEM((4, WIDTH // 4, L), F32),
            pltpu.VMEM((2, L, HP), BF16), pltpu.VMEM((2, 2, L, 2 * N), BF16), pltpu.VMEM((2, L, H), BF16),
            pltpu.VMEM((8, L), F32), pltpu.VMEM((4, 8, L), F32),
            pltpu.SemaphoreType.DMA((6,)), pltpu.SemaphoreType.DMA((7,)),
        ],
        comm=1,
    )(
        x_weight, bc_weight, dt_rows, x_paired, bc_paired, dt_paired, x, mixed, pre, bias, rate,
        carried, grown, states, g_x, g_mixed, g_read, g_write, layer_t,
    )
    return grad, saliency.reshape(L)


def solution(mesh):
    return jax.shard_map(
        shards,
        mesh=mesh,
        in_specs=(
            P("seq"), P("seq", None), P(), P(), P(None, "head"), P(), P(None, "head"), P("head"),
            P("head"), P("head"), P("seq", "head"),
        ),
        out_specs=(P("head", "seq"), P("seq")),
        check_vma=False,
    )
```

```python
import functools
import math

import jax
import jax.numpy as jnp
from jax import lax
from jax.experimental import pallas as pl
from jax.experimental.pallas import tpu as pltpu
from jax.sharding import PartitionSpec as P

L = 128
H = 8
HP = 512
N = 128
WIDTH = 2048
TILE = 256
F32 = jnp.float32
BF16 = jnp.bfloat16
NEG = -1e30
MESH = pl.DeviceIdType.MESH

NN = (((1,), (0,)), ((), ()))
NT = (((1,), (1,)), ((), ()))
TN = (((0,), (0,)), ((), ()))


def fast(a, b, dims=NN):
    return lax.dot_general(a.astype(BF16), b.astype(BF16), dims, preferred_element_type=F32)


def parts(a, terms=3):
    held = []
    for _ in range(terms):
        held.append(a.astype(BF16))
        a = a - held[-1].astype(F32)
    return held


def split(a, b, dims=NN, right=False):
    if right:
        a, b = a.astype(BF16), parts(b)
        return sum(lax.dot_general(a, p, dims, preferred_element_type=F32) for p in b)
    b = b.astype(BF16)
    return sum(lax.dot_general(p, b, dims, preferred_element_type=F32) for p in parts(a))


def split_right(a, b):
    return split(a, b, NN, True)


def iota(shape, axis):
    return lax.broadcasted_iota(jnp.int32, shape, axis)


def head_rows():
    return (iota((H, HP), 1) // 64 == iota((H, HP), 0)).astype(F32)


def reach(branch):
    row, col = iota((L, L), 0), iota((L, L), 1)
    return col <= row if branch == 0 else col >= row


def rates(pre, bias, rate):
    z = pre + bias
    stride = jnp.maximum(z, 0.0) + jnp.log1p(jnp.exp(-jnp.abs(z)))
    return z, stride, -rate * stride


def embed(tokens_row, embedding, residual):
    vocab = embedding.shape[0]
    hot = (iota((vocab, L), 0) == tokens_row).astype(F32).T.astype(BF16)
    return (
        jnp.dot(hot, embedding, preferred_element_type=F32) + residual.astype(F32)
    ).astype(BF16)


def local_grads(branch, x, mixed, stride, run, skip, ups):
    writer, reader = mixed[:, :N], mixed[:, N:]
    mask_t = reach(1 - branch)
    run_t = run.T
    spread = head_rows()
    low_half = iota((L, 2 * 64), 1) < 64
    scores_t = fast(writer, reader, NT)
    volume = jnp.zeros((L, L), F32)
    rows = []
    pieces = []
    for pair in range(H // 2):
        lanes = slice(128 * pair, 128 * pair + 128)
        x_pair, u_pair = x[:, lanes], ups[:, lanes]
        kernels, uppers = [], []
        for half in range(2):
            h = 2 * pair + half
            mine = low_half if half == 0 else jnp.logical_not(low_half)
            u_half = jnp.where(mine, u_pair, 0.0)
            fade = jnp.exp(jnp.where(mask_t, run_t[h : h + 1, :] - run[:, h : h + 1], NEG))
            cross = fast(x_pair, u_half, NT)
            weight = fade * cross * stride[:, h : h + 1]
            volume = volume + weight
            rows.append(jnp.sum(weight * scores_t, axis=0, keepdims=True))
            kernels.append((fade * scores_t).astype(BF16))
            uppers.append(u_half.astype(BF16))
        pieces.append(fast(jnp.concatenate(kernels, axis=1), jnp.concatenate(uppers, axis=0)))
    inner = jnp.concatenate(pieces, axis=1)
    d_inputs = split(skip, spread) * ups + split(stride, spread) * inner
    per_write = split(x * inner, spread.T)
    per_read = jnp.concatenate(rows, axis=0).T
    return d_inputs, fast(volume, reader), fast(volume.T, writer), per_read, per_write


def full_grads(
    branch, x, mixed, z, stride, run, rate, stride_e, decay_e, carried, grown, entry, later, local
):
    d_inputs, d_writer, d_reader, per_read, per_write = local
    writer, reader = mixed[:, :N], mixed[:, N:]
    total = run[L - 1 : L] if branch == 0 else run[0:1]
    spread = head_rows()
    spread_t = spread.T
    outer = decay_e * fast(writer, later, NT)
    d_inputs = d_inputs + stride_e * outer
    d_writer = d_writer + fast(carried, later)
    d_reader = d_reader + fast(grown, entry)
    written = split(x * outer, spread_t)
    per_write = per_write + written
    per_read = per_read + split(grown * fast(reader, entry, NT), spread_t)
    dots = split_right(spread, entry * later)
    overlap = split(jnp.ones((8, L), F32), dots, NT, True)[0:1]
    d_total = jnp.exp(total) * overlap + jnp.sum(stride * written, axis=0, keepdims=True)
    d_run = per_read - stride * per_write
    d_log = split_right(reach(1 - branch).astype(F32), d_run) + d_total
    d_stride = per_write - rate * d_log
    d_pre = d_stride / (1.0 + jnp.exp(-z))
    return d_inputs, d_pre, d_writer, d_reader


def project(source, x_weight, bc_weight, dt_rows):
    dot = functools.partial(jnp.dot, preferred_element_type=F32)
    pre = lax.dot_general(source, dt_rows, NT, preferred_element_type=F32)
    return dot(source, x_weight), dot(source, bc_weight), pre


def permutation(pairing_row, first, count, axis):
    shape = (WIDTH, count) if axis == 1 else (count, WIDTH)
    return (iota(shape, 0) + (0 if axis == 1 else first) == pairing_row).astype(F32).astype(BF16)


def padded_rows(factor, first):
    wide = jnp.broadcast_to(factor, (H, H))
    own = jnp.where(iota((H, H), 0) + first == iota((H, H), 1), wide, 0.0)
    return jnp.broadcast_to(jnp.sum(own, axis=1, keepdims=True), (H, N))


def kernel(
    tokens, residual, pairing, embedding, x_weight, bc_weight, dt_rows, bias, rate, skip, cotangent,
    grad, saliency,
    source, layer_t, ups, x, mixed, zs, strides, runs, stride_e, decay_e, carried, grown,
    g_x, g_mixed, g_read, g_write, x_paired, bc_paired, dt_paired,
    sums, factors, mate_in, mate_fac, chip, z_in, z_pre, x_in, y_in, e_out, e_in, far, far_in,
    x_fac, z_fac, states, d_x, d_mixed, d_pre, forward, part, got, sal_part, sal_got,
    send, recv, send_back, recv_back,
):
    seq, head = lax.axis_index("seq"), lax.axis_index("head")
    core = lax.rem(seq, 2)
    z = lax.rem(seq // 2, 4)
    xx = lax.rem(seq // 8, 4)
    yy = seq // 32

    def device(y_at, x_at, z_at, core_at):
        return (((y_at * 4 + x_at) * 4 + z_at) * 2 + core_at, head)

    def other(value, step):
        return lax.rem(value + step, 4)

    mate = device(yy, xx, z, 1 - core)
    z_peer = [device(yy, xx, other(z, d), core) for d in (1, 2, 3)]
    x_peer = [device(yy, other(xx, d), z, core) for d in (1, 2, 3)]
    y_peer = [device(other(yy, d), xx, z, core) for d in (1, 2, 3)]
    h_peer = [(seq, other(head, d)) for d in (1, 2, 3)]
    barrier = pltpu.get_barrier_semaphore()
    for peer in [mate] + z_peer + x_peer + y_peer + h_peer:
        pl.semaphore_signal(barrier, inc=1, device_id=peer, device_id_type=MESH)
    started = []

    def push(source_ref, target, slot, peer):
        copy = pltpu.make_async_remote_copy(
            src_ref=source_ref, dst_ref=target, send_sem=send.at[slot], recv_sem=recv.at[slot],
            device_id=peer, device_id_type=MESH,
        )
        copy.start()
        started.append(copy)
        return copy

    def place(j):
        return jnp.where(core == 0, j, 3 - j)

    def size(k):
        return pl.ds(0, 72 if k % 2 == 0 else 64)

    def front(branch, read):
        x_here, mixed_here, pre = project(read, x_weight[...], bc_weight[...], dt_rows[...])
        z_here, stride, log_decay = rates(pre, bias[...], rate[...])
        run = split_right(reach(branch).astype(F32), log_decay)
        total = jnp.sum(log_decay, axis=0, keepdims=True)
        spread = head_rows()
        fade = jnp.exp(total - run)
        x[branch] = x_here
        mixed[branch] = mixed_here
        zs[branch], strides[branch], runs[branch] = z_here, stride, run
        carry = x_here * split(fade * stride, spread)
        grow = ups[...] * split(jnp.exp(run), spread)
        end = fast(carry.T, mixed_here[:, :N])
        direct = fast(grow.T, mixed_here[:, N:])
        carried[branch] = carry.astype(BF16)
        grown[branch] = grow
        up, down = (end, direct) if branch == 0 else (direct, end)
        for way, value in ((0, up), (1, down)):
            for h in range(H):
                sums[way, 2 * branch + h % 2, h // 2] = value[64 * h : 64 * h + 64]
        for q in range(4):
            factors[branch, q] = padded_rows(jnp.exp(total), 2 * q)

    z_s, x_s, y_s, e_s, far_s = {}, {}, {}, {}, {}

    def pair(branch):
        ks = (2 * branch, 2 * branch + 1)
        mate_f = push(factors.at[branch], mate_fac.at[branch], branch, mate)
        mate_s = [push(sums.at[1 - core, k], mate_in.at[k], 2 + k, mate) for k in ks]
        mate_f.wait_recv()
        for k, arriving in zip(ks, mate_s):
            arriving.wait_recv()
            row = k % 2
            for q in range(4):
                chip[k, q, 0:64, :] = (
                    mate_fac[branch, q, row : row + 1, :] * sums[core, k, q] + mate_in[k, q]
                )
                if row == 0:
                    chip[k, q, 64:72, :] = mate_fac[branch, q] * factors[branch, q]
            z_s[k] = [
                push(chip.at[k, other(z, d), size(k)], z_in.at[k, z, size(k)], 5 + 3 * k + d, z_peer[d - 1])
                for d in (2, 1, 3)
            ]
            z_in[k, z] = chip[k, z]

    def z_step(k):
        for copy in z_s[k]:
            copy.wait_recv()
        even, row = k - k % 2, k % 2
        first = place(0)
        line = z_in[k, first, 0:64, :]
        factor = z_in[even, first, 64:72, :]
        for j in range(1, 4):
            spot = place(j)
            z_pre[k, spot] = line
            if row == 0:
                z_fac[k // 2, spot] = factor
                factor = factor * z_in[k, spot, 64:72, :]
            line = z_in[even, spot, 64 + row : 65 + row, :] * line + z_in[k, spot, 0:64, :]
        x_in[k, xx, 0:64, :] = line
        if row == 0:
            x_in[k, xx, 64:72, :] = factor
        x_s[k] = [
            push(x_in.at[k, xx, size(k)], x_in.at[k, xx, size(k)], 17 + 3 * k + d, x_peer[d - 1])
            for d in (1, 2, 3)
        ]

    def before(held, k, mine):
        even, row = k - k % 2, k % 2
        total, prefix = jnp.zeros((64, N), F32), jnp.zeros((64, N), F32)
        for j in range(4):
            spot = place(j)
            prefix = jnp.where(spot == mine, total, prefix)
            total = held[even, spot, 64 + row : 65 + row, :] * total + held[k, spot, 0:64, :]
        return prefix, total

    x_prefix = {}

    def x_step(k):
        for copy in x_s[k]:
            copy.wait_recv()
        x_prefix[k], total = before(x_in, k, xx)
        y_in[k, yy, 0:64, :] = total
        if k % 2 == 0:
            factor, prefix = jnp.ones((8, N), F32), jnp.ones((8, N), F32)
            for j in range(4):
                spot = place(j)
                prefix = jnp.where(spot == xx, factor, prefix)
                factor = factor * x_in[k, spot, 64:72, :]
            x_fac[k // 2] = prefix
            y_in[k, yy, 64:72, :] = factor
        y_s[k] = [
            push(y_in.at[k, yy, size(k)], y_in.at[k, yy, size(k)], 29 + 3 * k + d, y_peer[d - 1])
            for d in (1, 2, 3)
        ]

    def y_step(k):
        for copy in y_s[k]:
            copy.wait_recv()
        group, row = k // 2, k % 2
        y_prefix, _ = before(y_in, k, yy)
        line = x_fac[group, row : row + 1, :] * y_prefix + x_prefix[k]
        e_out[k, place(0)] = line
        for j in range(1, 4):
            spot = place(j)
            e_out[k, spot] = z_fac[group, spot, row : row + 1, :] * line + z_pre[k, spot]
        e_s[k] = [
            push(e_out.at[k, other(z, d)], e_in.at[k, z], 41 + 3 * k + d, z_peer[d - 1])
            for d in (2, 1, 3)
        ]
        e_in[k, z] = e_out[k, z]

    def alone(branch):
        d_in, d_w, d_r, per_read, per_write = local_grads(
            branch, x[branch], mixed[branch], strides[branch], runs[branch], skip[...], ups[...]
        )
        g_x[branch] = d_in
        g_mixed[branch, :, 0:N] = d_w
        g_mixed[branch, :, N : 2 * N] = d_r
        g_read[branch] = per_read
        g_write[branch] = per_write
        spread = head_rows()
        stride_e[branch] = split(strides[branch], spread)
        run = runs[branch]
        last = run[L - 1 : L] if branch == 0 else run[0:1]
        decay_e[branch] = split(jnp.exp(last - run), spread)

    def unpair(branch):
        ks = (2 * branch, 2 * branch + 1)
        for k in ks:
            for copy in e_s[k]:
                copy.wait_recv()
            row = k % 2
            for q in range(4):
                far[k, q] = factors[branch, q, row : row + 1, :] * e_in[k, q] + sums[core, k, q]
            far_s[k] = push(far.at[k], far_in.at[k], 54 + k, mate)
            states[core, k] = e_in[k]
        for k in ks:
            far_s[k].wait_recv()
            states[1 - core, k] = far_in[k]

    def joined(branch):
        way = (0, 1) if branch == 0 else (1, 0)

        def whole(direction):
            return jnp.concatenate(
                [states[direction, 2 * branch + h % 2, h // 2] for h in range(H)], axis=0
            )

        local = (
            g_x[branch], g_mixed[branch, :, 0:N], g_mixed[branch, :, N : 2 * N], g_read[branch],
            g_write[branch],
        )
        full_x, full_pre, g_writer, g_reader = full_grads(
            branch, x[branch], mixed[branch], zs[branch], strides[branch], runs[branch], rate[...],
            stride_e[branch], decay_e[branch], carried[branch], grown[branch], whole(way[0]),
            whole(way[1]), local,
        )
        d_x[branch] = full_x.astype(BF16)
        d_pre[branch] = full_pre.astype(BF16)
        for column, value in ((0, g_writer), (N, g_reader)):
            high = value.astype(BF16)
            d_mixed[branch, 0, :, column : column + N] = high
            d_mixed[branch, 1, :, column : column + N] = (value - high.astype(F32)).astype(BF16)

    def back(branch, weights, rows):
        dt_cols = weights[2][:, rows].astype(F32).T.astype(BF16)
        total = lax.dot_general(weights[0][rows, :], d_x[branch], NT, preferred_element_type=F32)
        for term in range(2):
            total = total + lax.dot_general(
                weights[1][rows, :], d_mixed[branch, term], NT, preferred_element_type=F32
            )
        return total + lax.dot_general(dt_cols, d_pre[branch], NT, preferred_element_type=F32)

    layer = embed(tokens[...], embedding[...], residual[...])
    ups[...] = cotangent[...].astype(F32)
    front(0, layer)
    pl.semaphore_wait(barrier, 13)
    pair(0)
    for block in range(WIDTH // TILE):
        cols = slice(TILE * block, TILE * block + TILE)
        hot = permutation(pairing[:, cols], 0, TILE, 1)
        source[:, cols] = jnp.dot(layer, hot, preferred_element_type=F32).astype(BF16)
    front(1, source[...])
    pair(1)
    @pl.loop(0, WIDTH // TILE)
    def _(block):
        rows = pl.ds(pl.multiple_of(block * TILE, TILE), TILE)
        hot = permutation(pairing[...], block * TILE, TILE, 0)
        for weight, target in ((x_weight, x_paired), (bc_weight, bc_paired)):
            target[rows, :] = jnp.dot(hot, weight[...], preferred_element_type=F32).astype(BF16)
        dt_paired[:, rows] = lax.dot_general(
            dt_rows[...], hot, NT, preferred_element_type=F32
        ).astype(BF16)

    z_step(0)
    z_step(1)
    x_step(0)
    y_step(0)
    z_step(2)
    x_step(1)
    y_step(1)
    z_step(3)
    x_step(2)
    y_step(2)
    x_step(3)
    y_step(3)
    layer_t[...] = layer.astype(F32).T.astype(BF16)
    alone(0)
    alone(1)
    unpair(0)
    joined(0)
    rows_here = WIDTH // 4
    for block in range(4):
        rows = slice(rows_here * block, rows_here * block + rows_here)
        forward[rows, :] = back(0, (x_weight, bc_weight, dt_rows), rows)
    unpair(1)
    joined(1)

    def chunk(owner):
        rows = pl.ds(pl.multiple_of(owner * rows_here, rows_here), rows_here)
        total = forward[rows, :] + back(1, (x_paired, bc_paired, dt_paired), rows)
        weighed = jnp.sum(total * layer_t[rows, :].astype(F32), axis=0, keepdims=True)
        return total, weighed

    def handover(source_ref, target, sent, slot, index):
        return pltpu.make_async_remote_copy(
            src_ref=source_ref, dst_ref=target, send_sem=send_back.at[sent], recv_sem=recv_back.at[slot],
            device_id=(seq, index), device_id_type=MESH,
        )

    def give(*route):
        copy = handover(*route)
        copy.start()
        started.append(copy)
        return copy

    def arrived(index):
        pltpu.make_async_remote_copy(
            src_ref=part.at[0], dst_ref=got.at[index], send_sem=send_back.at[0],
            recv_sem=recv_back.at[index], device_id=(seq, 3 - head), device_id_type=MESH,
        ).wait_recv()

    edge = jnp.logical_or(head == 0, head == 3)
    near = jnp.where(head < 2, 1, 2)
    second = jnp.where(head == 0, 2, jnp.where(head == 1, 0, jnp.where(head == 2, 3, 1)))
    third = jnp.where(head == 0, 1, jnp.where(head == 1, 3, jnp.where(head == 2, 0, 2)))
    slot = jnp.where(edge, 0, 1)
    total, weighed = chunk(3 - head)
    part[0] = total
    give(part.at[0], got.at[slot], 0, slot, jnp.where(edge, near, 3 - head))
    total, share = chunk(second)
    weighed = weighed + share
    part[1] = total
    give(part.at[1], got.at[2], 1, 2, second)
    total, share = chunk(third)
    weighed = weighed + share
    part[2] = total

    @pl.when(edge)
    def _():
        handover(part.at[2], got.at[3], 2, 3, third).start()

    total, share = chunk(head)
    weighed = weighed + share
    grad[...] = total
    sal_part[...] = jnp.broadcast_to(weighed, (8, L))
    sal_got[head] = sal_part[...]
    scan_sends = list(started[:-2])
    del started[:-2]
    shares = [
        give(sal_part, sal_got.at[head], 2 + d, 3 + d, h_peer[d - 1][1]) for d in (1, 2, 3)
    ]

    @pl.when(jnp.logical_not(edge))
    def _():
        arrived(0)
        part[2] = part[2] + got[0]
        handover(part.at[2], got.at[3], 2, 3, third).start()

    for copy in scan_sends:
        copy.wait_send()
    for copy in shares:
        copy.wait_recv()
    saliency[...] = (
        ((sal_got[0, 0:1] + sal_got[1, 0:1]) + sal_got[2, 0:1]) + sal_got[3, 0:1]
    ) / math.sqrt(WIDTH)

    @pl.when(jnp.logical_not(edge))
    def _():
        arrived(1)
        grad[...] = grad[...] + got[1]

    arrived(2)
    grad[...] = grad[...] + got[2]
    arrived(3)
    grad[...] = grad[...] + got[3]
    handover(part.at[2], got.at[3], 2, 3, third).wait_send()
    for copy in started:
        copy.wait_send()


VM = pl.BlockSpec(memory_space=pltpu.VMEM)


def final_kernel(grad, saliency, grad_out, saliency_out):
    grad_out[...] = grad[...]
    saliency_out[...] = saliency[...]


def shards(
    tokens, residual_in, pairing, embedding, x_weight, bc_weight, dt_weight, dt_bias, decay_rate,
    skip_gain, cotangent,
):
    tokens_row, pairing_row = tokens.reshape(1, L), pairing.reshape(1, WIDTH)
    bias, rate, skip = (value.reshape(1, H) for value in (dt_bias, decay_rate, skip_gain))
    shapes = [
        ((L, WIDTH), BF16), ((WIDTH, L), BF16), ((L, HP), F32), ((2, L, HP), F32),
        ((2, L, 2 * N), F32), ((2, L, H), F32), ((2, L, H), F32), ((2, L, H), F32),
        ((2, L, HP), F32), ((2, L, HP), F32), ((2, L, HP), BF16), ((2, L, HP), F32),
        ((2, L, HP), F32), ((2, L, 2 * N), F32), ((2, L, H), F32), ((2, L, H), F32),
        ((WIDTH, HP), BF16), ((WIDTH, 2 * N), BF16), ((H, WIDTH), BF16),
        ((2, 4, 4, 64, N), F32), ((2, 4, 8, N), F32), ((4, 4, 64, N), F32), ((2, 4, 8, N), F32),
        ((4, 4, 72, N), F32), ((4, 4, 72, N), F32), ((4, 4, 64, N), F32), ((4, 4, 72, N), F32),
        ((4, 4, 72, N), F32), ((4, 4, 64, N), F32), ((4, 4, 64, N), F32), ((4, 4, 64, N), F32),
        ((4, 4, 64, N), F32), ((2, 8, N), F32), ((2, 4, 8, N), F32), ((2, 4, 4, 64, N), F32),
        ((2, L, HP), BF16), ((2, 2, L, 2 * N), BF16), ((2, L, H), BF16), ((WIDTH, L), F32),
        ((3, WIDTH // 4, L), F32), ((4, WIDTH // 4, L), F32), ((8, L), F32), ((4, 8, L), F32),
    ]
    dma = pltpu.SemaphoreType.DMA
    grad, saliency = pl.pallas_call(
        kernel,
        out_shape=[
            jax.ShapeDtypeStruct((WIDTH // 4, L), F32), jax.ShapeDtypeStruct((1, L), F32),
        ],
        in_specs=[VM] * 11,
        out_specs=[VM] * 2,
        scratch_shapes=[pltpu.VMEM(*shape) for shape in shapes]
        + [dma((58,)), dma((58,)), dma((6,)), dma((7,))],
        compiler_params=pltpu.CompilerParams(
            collective_id=0, has_side_effects=True, vmem_limit_bytes=60 << 20
        ),
    )(
        tokens_row, residual_in, pairing_row, embedding, x_weight, bc_weight, dt_weight.T, bias, rate,
        skip, cotangent,
    )
    grad, saliency = pl.pallas_call(
        final_kernel,
        out_shape=[
            jax.ShapeDtypeStruct((WIDTH // 4, L), F32), jax.ShapeDtypeStruct((1, L), F32),
        ],
        in_specs=[VM] * 2,
        out_specs=[VM] * 2,
        compiler_params=pltpu.CompilerParams(vmem_limit_bytes=60 << 20),
    )(grad, saliency)
    return grad, saliency.reshape(L)


def solution(mesh):
    return jax.shard_map(
        shards,
        mesh=mesh,
        in_specs=(
            P("seq"), P("seq", None), P(), P(), P(None, "head"), P(), P(None, "head"), P("head"),
            P("head"), P("head"), P("seq", "head"),
        ),
        out_specs=(P("head", "seq"), P("seq")),
        check_vma=False,
    )
```

```python
import functools
import math

import jax
import jax.numpy as jnp
from jax import lax
from jax.experimental import pallas as pl
from jax.experimental.pallas import tpu as pltpu
from jax.sharding import PartitionSpec as P

L = 128
H = 8
HP = 512
N = 128
WIDTH = 2048
TILE = 256
F32 = jnp.float32
BF16 = jnp.bfloat16
NEG = -1e30
MESH = pl.DeviceIdType.MESH

NN = (((1,), (0,)), ((), ()))
NT = (((1,), (1,)), ((), ()))
TN = (((0,), (0,)), ((), ()))


def fast(a, b, dims=NN):
    return lax.dot_general(a.astype(BF16), b.astype(BF16), dims, preferred_element_type=F32)


def parts(a, terms=3):
    held = []
    for _ in range(terms):
        held.append(a.astype(BF16))
        a = a - held[-1].astype(F32)
    return held


def split(a, b, dims=NN, right=False):
    if right:
        a, b = a.astype(BF16), parts(b)
        return sum(lax.dot_general(a, p, dims, preferred_element_type=F32) for p in b)
    b = b.astype(BF16)
    return sum(lax.dot_general(p, b, dims, preferred_element_type=F32) for p in parts(a))


def split_right(a, b):
    return split(a, b, NN, True)


def iota(shape, axis):
    return lax.broadcasted_iota(jnp.int32, shape, axis)


def head_rows():
    return (iota((H, HP), 1) // 64 == iota((H, HP), 0)).astype(F32)


def reach(branch):
    row, col = iota((L, L), 0), iota((L, L), 1)
    return col <= row if branch == 0 else col >= row


def rates(pre, bias, rate):
    z = pre + bias
    stride = jnp.maximum(z, 0.0) + jnp.log1p(jnp.exp(-jnp.abs(z)))
    return z, stride, -rate * stride


def embed(tokens_row, embedding, residual):
    vocab = embedding.shape[0]
    hot = (iota((vocab, L), 0) == tokens_row).astype(F32).T.astype(BF16)
    return (
        jnp.dot(hot, embedding, preferred_element_type=F32) + residual.astype(F32)
    ).astype(BF16)


def local_grads(branch, x, mixed, stride, run, skip, ups):
    writer, reader = mixed[:, :N], mixed[:, N:]
    mask_t = reach(1 - branch)
    run_t = run.T
    spread = head_rows()
    low_half = iota((L, 2 * 64), 1) < 64
    scores_t = fast(writer, reader, NT)
    volume = jnp.zeros((L, L), F32)
    rows = []
    pieces = []
    for pair in range(H // 2):
        lanes = slice(128 * pair, 128 * pair + 128)
        x_pair, u_pair = x[:, lanes], ups[:, lanes]
        kernels, uppers = [], []
        for half in range(2):
            h = 2 * pair + half
            mine = low_half if half == 0 else jnp.logical_not(low_half)
            u_half = jnp.where(mine, u_pair, 0.0)
            fade = jnp.exp(jnp.where(mask_t, run_t[h : h + 1, :] - run[:, h : h + 1], NEG))
            cross = fast(x_pair, u_half, NT)
            weight = fade * cross * stride[:, h : h + 1]
            volume = volume + weight
            rows.append(jnp.sum(weight * scores_t, axis=0, keepdims=True))
            kernels.append((fade * scores_t).astype(BF16))
            uppers.append(u_half.astype(BF16))
        pieces.append(fast(jnp.concatenate(kernels, axis=1), jnp.concatenate(uppers, axis=0)))
    inner = jnp.concatenate(pieces, axis=1)
    d_inputs = split(skip, spread) * ups + split(stride, spread) * inner
    per_write = split(x * inner, spread.T)
    per_read = jnp.concatenate(rows, axis=0).T
    return d_inputs, fast(volume, reader), fast(volume.T, writer), per_read, per_write


def full_grads(
    branch, x, mixed, z, stride, run, rate, stride_e, decay_e, carried, grown, entry, later, local
):
    d_inputs, d_writer, d_reader, per_read, per_write = local
    writer, reader = mixed[:, :N], mixed[:, N:]
    total = run[L - 1 : L] if branch == 0 else run[0:1]
    spread = head_rows()
    spread_t = spread.T
    outer = decay_e * fast(writer, later, NT)
    d_inputs = d_inputs + stride_e * outer
    d_writer = d_writer + fast(carried, later)
    d_reader = d_reader + fast(grown, entry)
    written = split(x * outer, spread_t)
    per_write = per_write + written
    per_read = per_read + split(grown * fast(reader, entry, NT), spread_t)
    dots = split_right(spread, entry * later)
    overlap = split(jnp.ones((8, L), F32), dots, NT, True)[0:1]
    d_total = jnp.exp(total) * overlap + jnp.sum(stride * written, axis=0, keepdims=True)
    d_run = per_read - stride * per_write
    d_log = split_right(reach(1 - branch).astype(F32), d_run) + d_total
    d_stride = per_write - rate * d_log
    d_pre = d_stride / (1.0 + jnp.exp(-z))
    return d_inputs, d_pre, d_writer, d_reader


def project(source, x_weight, bc_weight, dt_rows):
    dot = functools.partial(jnp.dot, preferred_element_type=F32)
    pre = lax.dot_general(source, dt_rows, NT, preferred_element_type=F32)
    return dot(source, x_weight), dot(source, bc_weight), pre


def permutation(pairing_row, first, count, axis):
    shape = (WIDTH, count) if axis == 1 else (count, WIDTH)
    return (iota(shape, 0) + (0 if axis == 1 else first) == pairing_row).astype(F32).astype(BF16)


def padded_rows(factor, first):
    wide = jnp.broadcast_to(factor, (H, H))
    own = jnp.where(iota((H, H), 0) + first == iota((H, H), 1), wide, 0.0)
    return jnp.broadcast_to(jnp.sum(own, axis=1, keepdims=True), (H, N))


def kernel(
    tokens, residual, pairing, embedding, x_weight, bc_weight, dt_rows, bias, rate, skip, cotangent,
    grad, saliency,
    source, layer_t, ups, x, mixed, zs, strides, runs, stride_e, decay_e, carried, grown,
    g_x, g_mixed, g_read, g_write, x_paired, bc_paired, dt_paired,
    sums, factors, mate_in, mate_fac, chip, z_in, z_pre, x_in, y_in, e_out, e_in, far, far_in,
    x_fac, z_fac, states, d_x, d_mixed, d_pre, forward, part, got, sal_part, sal_got,
    send, recv, send_back, recv_back,
):
    seq, head = lax.axis_index("seq"), lax.axis_index("head")
    core = lax.rem(seq, 2)
    z = lax.rem(seq // 2, 4)
    xx = lax.rem(seq // 8, 4)
    yy = seq // 32

    def device(y_at, x_at, z_at, core_at):
        return (((y_at * 4 + x_at) * 4 + z_at) * 2 + core_at, head)

    def other(value, step):
        return lax.rem(value + step, 4)

    mate = device(yy, xx, z, 1 - core)
    z_peer = [device(yy, xx, other(z, d), core) for d in (1, 2, 3)]
    x_peer = [device(yy, other(xx, d), z, core) for d in (1, 2, 3)]
    y_peer = [device(other(yy, d), xx, z, core) for d in (1, 2, 3)]
    h_peer = [(seq, other(head, d)) for d in (1, 2, 3)]
    barrier = pltpu.get_barrier_semaphore()
    for peer in [mate] + z_peer + x_peer + y_peer + h_peer:
        pl.semaphore_signal(barrier, inc=1, device_id=peer, device_id_type=MESH)
    started = []

    def push(source_ref, target, slot, peer):
        copy = pltpu.make_async_remote_copy(
            src_ref=source_ref, dst_ref=target, send_sem=send.at[slot], recv_sem=recv.at[slot],
            device_id=peer, device_id_type=MESH,
        )
        copy.start()
        started.append(copy)
        return copy

    def place(j):
        return jnp.where(core == 0, j, 3 - j)

    def size(k):
        return pl.ds(0, 72 if k % 2 == 0 else 64)

    def front(branch, read):
        x_here, mixed_here, pre = project(read, x_weight[...], bc_weight[...], dt_rows[...])
        z_here, stride, log_decay = rates(pre, bias[...], rate[...])
        run = split_right(reach(branch).astype(F32), log_decay)
        total = jnp.sum(log_decay, axis=0, keepdims=True)
        spread = head_rows()
        fade = jnp.exp(total - run)
        x[branch] = x_here
        mixed[branch] = mixed_here
        zs[branch], strides[branch], runs[branch] = z_here, stride, run
        carry = x_here * split(fade * stride, spread)
        grow = ups[...] * split(jnp.exp(run), spread)
        end = fast(carry.T, mixed_here[:, :N])
        direct = fast(grow.T, mixed_here[:, N:])
        carried[branch] = carry.astype(BF16)
        grown[branch] = grow
        up, down = (end, direct) if branch == 0 else (direct, end)
        for way, value in ((0, up), (1, down)):
            for h in range(H):
                sums[way, 2 * branch + h % 2, h // 2] = value[64 * h : 64 * h + 64]
        for q in range(4):
            factors[branch, q] = padded_rows(jnp.exp(total), 2 * q)

    z_s, x_s, y_s, e_s, far_s = {}, {}, {}, {}, {}

    def pair(branch):
        ks = (2 * branch, 2 * branch + 1)
        mate_f = push(factors.at[branch], mate_fac.at[branch], branch, mate)
        mate_s = [push(sums.at[1 - core, k], mate_in.at[k], 2 + k, mate) for k in ks]
        mate_f.wait_recv()
        for k, arriving in zip(ks, mate_s):
            arriving.wait_recv()
            row = k % 2
            for q in range(4):
                chip[k, q, 0:64, :] = (
                    mate_fac[branch, q, row : row + 1, :] * sums[core, k, q] + mate_in[k, q]
                )
                if row == 0:
                    chip[k, q, 64:72, :] = mate_fac[branch, q] * factors[branch, q]
            z_s[k] = [
                push(chip.at[k, other(z, d), size(k)], z_in.at[k, z, size(k)], 5 + 3 * k + d, z_peer[d - 1])
                for d in (2, 1, 3)
            ]
            z_in[k, z] = chip[k, z]

    def z_step(k):
        for copy in z_s[k]:
            copy.wait_recv()
        even, row = k - k % 2, k % 2
        first = place(0)
        line = z_in[k, first, 0:64, :]
        factor = z_in[even, first, 64:72, :]
        for j in range(1, 4):
            spot = place(j)
            z_pre[k, spot] = line
            if row == 0:
                z_fac[k // 2, spot] = factor
                factor = factor * z_in[k, spot, 64:72, :]
            line = z_in[even, spot, 64 + row : 65 + row, :] * line + z_in[k, spot, 0:64, :]
        x_in[k, xx, 0:64, :] = line
        if row == 0:
            x_in[k, xx, 64:72, :] = factor
        x_s[k] = [
            push(x_in.at[k, xx, size(k)], x_in.at[k, xx, size(k)], 17 + 3 * k + d, x_peer[d - 1])
            for d in (1, 2, 3)
        ]

    def before(held, k, mine):
        even, row = k - k % 2, k % 2
        total, prefix = jnp.zeros((64, N), F32), jnp.zeros((64, N), F32)
        for j in range(4):
            spot = place(j)
            prefix = jnp.where(spot == mine, total, prefix)
            total = held[even, spot, 64 + row : 65 + row, :] * total + held[k, spot, 0:64, :]
        return prefix, total

    x_prefix = {}

    def x_step(k):
        for copy in x_s[k]:
            copy.wait_recv()
        x_prefix[k], total = before(x_in, k, xx)
        y_in[k, yy, 0:64, :] = total
        if k % 2 == 0:
            factor, prefix = jnp.ones((8, N), F32), jnp.ones((8, N), F32)
            for j in range(4):
                spot = place(j)
                prefix = jnp.where(spot == xx, factor, prefix)
                factor = factor * x_in[k, spot, 64:72, :]
            x_fac[k // 2] = prefix
            y_in[k, yy, 64:72, :] = factor
        y_s[k] = [
            push(y_in.at[k, yy, size(k)], y_in.at[k, yy, size(k)], 29 + 3 * k + d, y_peer[d - 1])
            for d in (1, 2, 3)
        ]

    def y_step(k):
        for copy in y_s[k]:
            copy.wait_recv()
        group, row = k // 2, k % 2
        y_prefix, _ = before(y_in, k, yy)
        line = x_fac[group, row : row + 1, :] * y_prefix + x_prefix[k]
        e_out[k, place(0)] = line
        for j in range(1, 4):
            spot = place(j)
            e_out[k, spot] = z_fac[group, spot, row : row + 1, :] * line + z_pre[k, spot]
        e_s[k] = [
            push(e_out.at[k, other(z, d)], e_in.at[k, z], 41 + 3 * k + d, z_peer[d - 1])
            for d in (2, 1, 3)
        ]
        e_in[k, z] = e_out[k, z]

    def alone(branch):
        d_in, d_w, d_r, per_read, per_write = local_grads(
            branch, x[branch], mixed[branch], strides[branch], runs[branch], skip[...], ups[...]
        )
        g_x[branch] = d_in
        g_mixed[branch, :, 0:N] = d_w
        g_mixed[branch, :, N : 2 * N] = d_r
        g_read[branch] = per_read
        g_write[branch] = per_write
        spread = head_rows()
        stride_e[branch] = split(strides[branch], spread)
        run = runs[branch]
        last = run[L - 1 : L] if branch == 0 else run[0:1]
        decay_e[branch] = split(jnp.exp(last - run), spread)

    def unpair(branch):
        ks = (2 * branch, 2 * branch + 1)
        for k in ks:
            for copy in e_s[k]:
                copy.wait_recv()
            row = k % 2
            for q in range(4):
                far[k, q] = factors[branch, q, row : row + 1, :] * e_in[k, q] + sums[core, k, q]
            far_s[k] = push(far.at[k], far_in.at[k], 54 + k, mate)
            states[core, k] = e_in[k]
        for k in ks:
            far_s[k].wait_recv()
            states[1 - core, k] = far_in[k]

    def joined(branch):
        way = (0, 1) if branch == 0 else (1, 0)

        def whole(direction):
            return jnp.concatenate(
                [states[direction, 2 * branch + h % 2, h // 2] for h in range(H)], axis=0
            )

        local = (
            g_x[branch], g_mixed[branch, :, 0:N], g_mixed[branch, :, N : 2 * N], g_read[branch],
            g_write[branch],
        )
        full_x, full_pre, g_writer, g_reader = full_grads(
            branch, x[branch], mixed[branch], zs[branch], strides[branch], runs[branch], rate[...],
            stride_e[branch], decay_e[branch], carried[branch], grown[branch], whole(way[0]),
            whole(way[1]), local,
        )
        d_x[branch] = full_x.astype(BF16)
        d_pre[branch] = full_pre.astype(BF16)
        for column, value in ((0, g_writer), (N, g_reader)):
            high = value.astype(BF16)
            d_mixed[branch, 0, :, column : column + N] = high
            d_mixed[branch, 1, :, column : column + N] = (value - high.astype(F32)).astype(BF16)

    def back(branch, weights, rows):
        dt_cols = weights[2][:, rows].astype(F32).T.astype(BF16)
        total = lax.dot_general(weights[0][rows, :], d_x[branch], NT, preferred_element_type=F32)
        for term in range(2):
            total = total + lax.dot_general(
                weights[1][rows, :], d_mixed[branch, term], NT, preferred_element_type=F32
            )
        return total + lax.dot_general(dt_cols, d_pre[branch], NT, preferred_element_type=F32)

    layer = embed(tokens[...], embedding[...], residual[...])
    ups[...] = cotangent[...].astype(F32)
    front(0, layer)
    pl.semaphore_wait(barrier, 13)
    pair(0)
    for block in range(WIDTH // TILE):
        cols = slice(TILE * block, TILE * block + TILE)
        hot = permutation(pairing[:, cols], 0, TILE, 1)
        source[:, cols] = jnp.dot(layer, hot, preferred_element_type=F32).astype(BF16)
    front(1, source[...])
    pair(1)
    @pl.loop(0, WIDTH // TILE)
    def _(block):
        rows = pl.ds(pl.multiple_of(block * TILE, TILE), TILE)
        hot = permutation(pairing[...], block * TILE, TILE, 0)
        for weight, target in ((x_weight, x_paired), (bc_weight, bc_paired)):
            target[rows, :] = jnp.dot(hot, weight[...], preferred_element_type=F32).astype(BF16)
        dt_paired[:, rows] = lax.dot_general(
            dt_rows[...], hot, NT, preferred_element_type=F32
        ).astype(BF16)

    z_step(0)
    z_step(1)
    x_step(0)
    y_step(0)
    z_step(2)
    x_step(1)
    y_step(1)
    z_step(3)
    x_step(2)
    y_step(2)
    x_step(3)
    y_step(3)
    layer_t[...] = layer.astype(F32).T.astype(BF16)
    alone(0)
    alone(1)
    unpair(0)
    joined(0)
    rows_here = WIDTH // 4
    for block in range(4):
        rows = slice(rows_here * block, rows_here * block + rows_here)
        forward[rows, :] = back(0, (x_weight, bc_weight, dt_rows), rows)
    unpair(1)
    joined(1)

    def chunk(owner):
        rows = pl.ds(pl.multiple_of(owner * rows_here, rows_here), rows_here)
        total = forward[rows, :] + back(1, (x_paired, bc_paired, dt_paired), rows)
        weighed = jnp.sum(total * layer_t[rows, :].astype(F32), axis=0, keepdims=True)
        return total, weighed

    def handover(source_ref, target, sent, slot, index):
        return pltpu.make_async_remote_copy(
            src_ref=source_ref, dst_ref=target, send_sem=send_back.at[sent], recv_sem=recv_back.at[slot],
            device_id=(seq, index), device_id_type=MESH,
        )

    def give(*route):
        copy = handover(*route)
        copy.start()
        started.append(copy)
        return copy

    def arrived(index):
        pltpu.make_async_remote_copy(
            src_ref=part.at[0], dst_ref=got.at[index], send_sem=send_back.at[0],
            recv_sem=recv_back.at[index], device_id=(seq, 3 - head), device_id_type=MESH,
        ).wait_recv()

    edge = jnp.logical_or(head == 0, head == 3)
    near = jnp.where(head < 2, 1, 2)
    second = jnp.where(head == 0, 2, jnp.where(head == 1, 0, jnp.where(head == 2, 3, 1)))
    third = jnp.where(head == 0, 1, jnp.where(head == 1, 3, jnp.where(head == 2, 0, 2)))
    slot = jnp.where(edge, 0, 1)
    total, weighed = chunk(3 - head)
    part[0] = total
    route = [
        (part.at[0], got.at[slot], 0, slot, jnp.where(edge, near, 3 - head)),
        (part.at[1], got.at[2], 1, 2, second),
        (part.at[2], got.at[3], 2, 3, third),
    ]
    handover(*route[0]).start()
    total, share = chunk(second)
    weighed = weighed + share
    part[1] = total

    @pl.when(jnp.logical_not(edge))
    def _():
        handover(*route[1]).start()

    total, share = chunk(third)
    weighed = weighed + share
    part[2] = total
    total, share = chunk(head)
    weighed = weighed + share
    grad[...] = total
    sal_part[...] = jnp.broadcast_to(weighed, (8, L))
    sal_got[head] = sal_part[...]
    scan_sends = list(started)
    del started[:]
    shares = [
        give(sal_part, sal_got.at[head], 2 + d, 3 + d, h_peer[d - 1][1]) for d in (1, 2, 3)
    ]

    @pl.when(edge)
    def _():
        handover(*route[0]).wait_send()
        handover(*route[1]).start()
        handover(*route[2]).start()

    @pl.when(jnp.logical_not(edge))
    def _():
        arrived(0)
        part[2] = part[2] + got[0]
        handover(*route[2]).start()
        handover(*route[0]).wait_send()

    for copy in scan_sends:
        copy.wait_send()
    for copy in shares:
        copy.wait_recv()
    saliency[...] = (
        ((sal_got[0, 0:1] + sal_got[1, 0:1]) + sal_got[2, 0:1]) + sal_got[3, 0:1]
    ) / math.sqrt(WIDTH)

    @pl.when(jnp.logical_not(edge))
    def _():
        arrived(1)
        grad[...] = grad[...] + got[1]

    arrived(2)
    grad[...] = grad[...] + got[2]
    arrived(3)
    grad[...] = grad[...] + got[3]
    handover(*route[1]).wait_send()
    handover(*route[2]).wait_send()
    for copy in started:
        copy.wait_send()


VM = pl.BlockSpec(memory_space=pltpu.VMEM)


def final_kernel(grad, saliency, grad_out, saliency_out):
    grad_out[...] = grad[...]
    saliency_out[...] = saliency[...]


def shards(
    tokens, residual_in, pairing, embedding, x_weight, bc_weight, dt_weight, dt_bias, decay_rate,
    skip_gain, cotangent,
):
    tokens_row, pairing_row = tokens.reshape(1, L), pairing.reshape(1, WIDTH)
    bias, rate, skip = (value.reshape(1, H) for value in (dt_bias, decay_rate, skip_gain))
    shapes = [
        ((L, WIDTH), BF16), ((WIDTH, L), BF16), ((L, HP), F32), ((2, L, HP), F32),
        ((2, L, 2 * N), F32), ((2, L, H), F32), ((2, L, H), F32), ((2, L, H), F32),
        ((2, L, HP), F32), ((2, L, HP), F32), ((2, L, HP), BF16), ((2, L, HP), F32),
        ((2, L, HP), F32), ((2, L, 2 * N), F32), ((2, L, H), F32), ((2, L, H), F32),
        ((WIDTH, HP), BF16), ((WIDTH, 2 * N), BF16), ((H, WIDTH), BF16),
        ((2, 4, 4, 64, N), F32), ((2, 4, 8, N), F32), ((4, 4, 64, N), F32), ((2, 4, 8, N), F32),
        ((4, 4, 72, N), F32), ((4, 4, 72, N), F32), ((4, 4, 64, N), F32), ((4, 4, 72, N), F32),
        ((4, 4, 72, N), F32), ((4, 4, 64, N), F32), ((4, 4, 64, N), F32), ((4, 4, 64, N), F32),
        ((4, 4, 64, N), F32), ((2, 8, N), F32), ((2, 4, 8, N), F32), ((2, 4, 4, 64, N), F32),
        ((2, L, HP), BF16), ((2, 2, L, 2 * N), BF16), ((2, L, H), BF16), ((WIDTH, L), F32),
        ((3, WIDTH // 4, L), F32), ((4, WIDTH // 4, L), F32), ((8, L), F32), ((4, 8, L), F32),
    ]
    dma = pltpu.SemaphoreType.DMA
    grad, saliency = pl.pallas_call(
        kernel,
        out_shape=[
            jax.ShapeDtypeStruct((WIDTH // 4, L), F32), jax.ShapeDtypeStruct((1, L), F32),
        ],
        in_specs=[VM] * 11,
        out_specs=[VM] * 2,
        scratch_shapes=[pltpu.VMEM(*shape) for shape in shapes]
        + [dma((58,)), dma((58,)), dma((6,)), dma((7,))],
        compiler_params=pltpu.CompilerParams(
            collective_id=0, has_side_effects=True, vmem_limit_bytes=60 << 20
        ),
    )(
        tokens_row, residual_in, pairing_row, embedding, x_weight, bc_weight, dt_weight.T, bias, rate,
        skip, cotangent,
    )
    grad, saliency = pl.pallas_call(
        final_kernel,
        out_shape=[
            jax.ShapeDtypeStruct((WIDTH // 4, L), F32), jax.ShapeDtypeStruct((1, L), F32),
        ],
        in_specs=[VM] * 2,
        out_specs=[VM] * 2,
        compiler_params=pltpu.CompilerParams(vmem_limit_bytes=60 << 20),
    )(grad, saliency)
    return grad, saliency.reshape(L)


def solution(mesh):
    return jax.shard_map(
        shards,
        mesh=mesh,
        in_specs=(
            P("seq"), P("seq", None), P(), P(), P(None, "head"), P(), P(None, "head"), P("head"),
            P("head"), P("head"), P("seq", "head"),
        ),
        out_specs=(P("head", "seq"), P("seq")),
        check_vma=False,
    )
```

```python
import functools
import math

import jax
import jax.numpy as jnp
from jax import lax
from jax.experimental import pallas as pl
from jax.experimental.pallas import tpu as pltpu
from jax.sharding import PartitionSpec as P

L = 128
H = 8
HP = 512
N = 128
WIDTH = 2048
TILE = 256
F32 = jnp.float32
BF16 = jnp.bfloat16
NEG = -1e30
MESH = pl.DeviceIdType.MESH

NN = (((1,), (0,)), ((), ()))
NT = (((1,), (1,)), ((), ()))
TN = (((0,), (0,)), ((), ()))


def fast(a, b, dims=NN):
    return lax.dot_general(a.astype(BF16), b.astype(BF16), dims, preferred_element_type=F32)


def parts(a, terms=3):
    held = []
    for _ in range(terms):
        held.append(a.astype(BF16))
        a = a - held[-1].astype(F32)
    return held


def split(a, b, dims=NN, right=False):
    if right:
        a, b = a.astype(BF16), parts(b)
        return sum(lax.dot_general(a, p, dims, preferred_element_type=F32) for p in b)
    b = b.astype(BF16)
    return sum(lax.dot_general(p, b, dims, preferred_element_type=F32) for p in parts(a))


def split_right(a, b):
    return split(a, b, NN, True)


def iota(shape, axis):
    return lax.broadcasted_iota(jnp.int32, shape, axis)


def head_rows():
    return (iota((H, HP), 1) // 64 == iota((H, HP), 0)).astype(F32)


def reach(branch):
    row, col = iota((L, L), 0), iota((L, L), 1)
    return col <= row if branch == 0 else col >= row


def rates(pre, bias, rate):
    z = pre + bias
    stride = jnp.maximum(z, 0.0) + jnp.log1p(jnp.exp(-jnp.abs(z)))
    return z, stride, -rate * stride


def embed(tokens_row, embedding, residual):
    vocab = embedding.shape[0]
    hot = (iota((vocab, L), 0) == tokens_row).astype(F32).T.astype(BF16)
    return (
        jnp.dot(hot, embedding, preferred_element_type=F32) + residual.astype(F32)
    ).astype(BF16)


def local_grads(branch, x, mixed, stride, run, skip, ups):
    writer, reader = mixed[:, :N], mixed[:, N:]
    mask_t = reach(1 - branch)
    run_t = run.T
    spread = head_rows()
    low_half = iota((L, 2 * 64), 1) < 64
    scores_t = fast(writer, reader, NT)
    volume = jnp.zeros((L, L), F32)
    rows = []
    pieces = []
    for pair in range(H // 2):
        lanes = slice(128 * pair, 128 * pair + 128)
        x_pair, u_pair = x[:, lanes], ups[:, lanes]
        kernels, uppers = [], []
        for half in range(2):
            h = 2 * pair + half
            mine = low_half if half == 0 else jnp.logical_not(low_half)
            u_half = jnp.where(mine, u_pair, 0.0)
            fade = jnp.exp(jnp.where(mask_t, run_t[h : h + 1, :] - run[:, h : h + 1], NEG))
            cross = fast(x_pair, u_half, NT)
            weight = fade * cross * stride[:, h : h + 1]
            volume = volume + weight
            rows.append(jnp.sum(weight * scores_t, axis=0, keepdims=True))
            kernels.append((fade * scores_t).astype(BF16))
            uppers.append(u_half.astype(BF16))
        pieces.append(fast(jnp.concatenate(kernels, axis=1), jnp.concatenate(uppers, axis=0)))
    inner = jnp.concatenate(pieces, axis=1)
    d_inputs = split(skip, spread) * ups + split(stride, spread) * inner
    per_write = split(x * inner, spread.T)
    per_read = jnp.concatenate(rows, axis=0).T
    return d_inputs, fast(volume, reader), fast(volume.T, writer), per_read, per_write


def full_grads(
    branch, x, mixed, z, stride, run, rate, stride_e, decay_e, carried, grown, entry, later, local
):
    d_inputs, d_writer, d_reader, per_read, per_write = local
    writer, reader = mixed[:, :N], mixed[:, N:]
    total = run[L - 1 : L] if branch == 0 else run[0:1]
    spread = head_rows()
    spread_t = spread.T
    outer = decay_e * fast(writer, later, NT)
    d_inputs = d_inputs + stride_e * outer
    d_writer = d_writer + fast(carried, later)
    d_reader = d_reader + fast(grown, entry)
    written = split(x * outer, spread_t)
    per_write = per_write + written
    per_read = per_read + split(grown * fast(reader, entry, NT), spread_t)
    dots = split_right(spread, entry * later)
    overlap = split(jnp.ones((8, L), F32), dots, NT, True)[0:1]
    d_total = jnp.exp(total) * overlap + jnp.sum(stride * written, axis=0, keepdims=True)
    d_run = per_read - stride * per_write
    d_log = split_right(reach(1 - branch).astype(F32), d_run) + d_total
    d_stride = per_write - rate * d_log
    d_pre = d_stride / (1.0 + jnp.exp(-z))
    return d_inputs, d_pre, d_writer, d_reader


def project(source, x_weight, bc_weight, dt_rows):
    dot = functools.partial(jnp.dot, preferred_element_type=F32)
    pre = lax.dot_general(source, dt_rows, NT, preferred_element_type=F32)
    return dot(source, x_weight), dot(source, bc_weight), pre


def permutation(pairing_row, first, count, axis):
    shape = (WIDTH, count) if axis == 1 else (count, WIDTH)
    return (iota(shape, 0) + (0 if axis == 1 else first) == pairing_row).astype(F32).astype(BF16)


def padded_rows(factor, first):
    wide = jnp.broadcast_to(factor, (H, H))
    own = jnp.where(iota((H, H), 0) + first == iota((H, H), 1), wide, 0.0)
    return jnp.broadcast_to(jnp.sum(own, axis=1, keepdims=True), (H, N))


def kernel(
    tokens, residual_far, pairing, embedding, x_far, bc_far, dt_rows, bias, rate, skip, cotangent_far,
    grad, saliency,
    residual, x_weight, bc_weight, cotangent, load, source, layer_t, ups, x, mixed, zs, strides, runs, stride_e, decay_e, carried, grown,
    g_x, g_mixed, g_read, g_write, x_paired, bc_paired, dt_paired,
    sums, factors, mate_in, mate_fac, chip, z_in, z_pre, x_in, y_in, e_out, e_in, far, far_in,
    x_fac, z_fac, states, d_x, d_mixed, d_pre, forward, part, got, sal_part, sal_got,
    send, recv, send_back, recv_back,
):
    seq, head = lax.axis_index("seq"), lax.axis_index("head")
    core = lax.rem(seq, 2)
    z = lax.rem(seq // 2, 4)
    xx = lax.rem(seq // 8, 4)
    yy = seq // 32

    def device(y_at, x_at, z_at, core_at):
        return (((y_at * 4 + x_at) * 4 + z_at) * 2 + core_at, head)

    def other(value, step):
        return lax.rem(value + step, 4)

    mate = device(yy, xx, z, 1 - core)
    z_peer = [device(yy, xx, other(z, d), core) for d in (1, 2, 3)]
    x_peer = [device(yy, other(xx, d), z, core) for d in (1, 2, 3)]
    y_peer = [device(other(yy, d), xx, z, core) for d in (1, 2, 3)]
    h_peer = [(seq, other(head, d)) for d in (1, 2, 3)]
    barrier = pltpu.get_barrier_semaphore()
    for peer in z_peer + y_peer + x_peer + h_peer + [mate]:
        pl.semaphore_signal(barrier, inc=1, device_id=peer, device_id_type=MESH)
    loads = [
        pltpu.make_async_copy(source_ref, target, load.at[index])
        for index, (source_ref, target) in enumerate((
            (residual_far, residual), (x_far, x_weight), (bc_far, bc_weight), (cotangent_far, cotangent)
        ))
    ]
    for copy in loads:
        copy.start()
    started = []

    def push(source_ref, target, slot, peer):
        copy = pltpu.make_async_remote_copy(
            src_ref=source_ref, dst_ref=target, send_sem=send.at[slot], recv_sem=recv.at[slot],
            device_id=peer, device_id_type=MESH,
        )
        copy.start()
        started.append(copy)
        return copy

    def place(j):
        return jnp.where(core == 0, j, 3 - j)

    def size(k):
        return pl.ds(0, 72 if k % 2 == 0 else 64)

    def front(branch, read):
        x_here, mixed_here, pre = project(read, x_weight[...], bc_weight[...], dt_rows[...])
        z_here, stride, log_decay = rates(pre, bias[...], rate[...])
        run = split_right(reach(branch).astype(F32), log_decay)
        total = jnp.sum(log_decay, axis=0, keepdims=True)
        spread = head_rows()
        fade = jnp.exp(total - run)
        x[branch] = x_here
        mixed[branch] = mixed_here
        zs[branch], strides[branch], runs[branch] = z_here, stride, run
        carry = x_here * split(fade * stride, spread)
        grow = ups[...] * split(jnp.exp(run), spread)
        end = fast(carry.T, mixed_here[:, :N])
        direct = fast(grow.T, mixed_here[:, N:])
        carried[branch] = carry.astype(BF16)
        grown[branch] = grow
        up, down = (end, direct) if branch == 0 else (direct, end)
        for way, value in ((0, up), (1, down)):
            for h in range(H):
                sums[way, 2 * branch + h % 2, h // 2] = value[64 * h : 64 * h + 64]
        for q in range(4):
            factors[branch, q] = padded_rows(jnp.exp(total), 2 * q)

    z_s, x_s, y_s, e_s, far_s = {}, {}, {}, {}, {}

    def pair(branch):
        ks = (2 * branch, 2 * branch + 1)
        mate_f = push(factors.at[branch], mate_fac.at[branch], branch, mate)
        mate_s = [push(sums.at[1 - core, k], mate_in.at[k], 2 + k, mate) for k in ks]
        mate_f.wait_recv()
        for k, arriving in zip(ks, mate_s):
            arriving.wait_recv()
            row = k % 2
            for q in range(4):
                chip[k, q, 0:64, :] = (
                    mate_fac[branch, q, row : row + 1, :] * sums[core, k, q] + mate_in[k, q]
                )
                if row == 0:
                    chip[k, q, 64:72, :] = mate_fac[branch, q] * factors[branch, q]
            z_s[k] = [
                push(chip.at[k, other(z, d), size(k)], z_in.at[k, z, size(k)], 5 + 3 * k + d, z_peer[d - 1])
                for d in (2, 1, 3)
            ]
            z_in[k, z] = chip[k, z]

    def z_step(k):
        for copy in z_s[k]:
            copy.wait_recv()
        even, row = k - k % 2, k % 2
        first = place(0)
        line = z_in[k, first, 0:64, :]
        factor = z_in[even, first, 64:72, :]
        for j in range(1, 4):
            spot = place(j)
            z_pre[k, spot] = line
            if row == 0:
                z_fac[k // 2, spot] = factor
                factor = factor * z_in[k, spot, 64:72, :]
            line = z_in[even, spot, 64 + row : 65 + row, :] * line + z_in[k, spot, 0:64, :]
        x_in[k, xx, 0:64, :] = line
        if row == 0:
            x_in[k, xx, 64:72, :] = factor
        x_s[k] = [
            push(x_in.at[k, xx, size(k)], x_in.at[k, xx, size(k)], 17 + 3 * k + d, x_peer[d - 1])
            for d in (1, 2, 3)
        ]

    def before(held, k, mine):
        even, row = k - k % 2, k % 2
        total, prefix = jnp.zeros((64, N), F32), jnp.zeros((64, N), F32)
        for j in range(4):
            spot = place(j)
            prefix = jnp.where(spot == mine, total, prefix)
            total = held[even, spot, 64 + row : 65 + row, :] * total + held[k, spot, 0:64, :]
        return prefix, total

    x_prefix = {}

    def x_step(k):
        for copy in x_s[k]:
            copy.wait_recv()
        x_prefix[k], total = before(x_in, k, xx)
        y_in[k, yy, 0:64, :] = total
        if k % 2 == 0:
            factor, prefix = jnp.ones((8, N), F32), jnp.ones((8, N), F32)
            for j in range(4):
                spot = place(j)
                prefix = jnp.where(spot == xx, factor, prefix)
                factor = factor * x_in[k, spot, 64:72, :]
            x_fac[k // 2] = prefix
            y_in[k, yy, 64:72, :] = factor
        y_s[k] = [
            push(y_in.at[k, yy, size(k)], y_in.at[k, yy, size(k)], 29 + 3 * k + d, y_peer[d - 1])
            for d in (1, 2, 3)
        ]

    def y_step(k):
        for copy in y_s[k]:
            copy.wait_recv()
        group, row = k // 2, k % 2
        y_prefix, _ = before(y_in, k, yy)
        line = x_fac[group, row : row + 1, :] * y_prefix + x_prefix[k]
        e_out[k, place(0)] = line
        for j in range(1, 4):
            spot = place(j)
            e_out[k, spot] = z_fac[group, spot, row : row + 1, :] * line + z_pre[k, spot]
        e_s[k] = [
            push(e_out.at[k, other(z, d)], e_in.at[k, z], 41 + 3 * k + d, z_peer[d - 1])
            for d in (2, 1, 3)
        ]
        e_in[k, z] = e_out[k, z]

    def alone(branch):
        d_in, d_w, d_r, per_read, per_write = local_grads(
            branch, x[branch], mixed[branch], strides[branch], runs[branch], skip[...], ups[...]
        )
        g_x[branch] = d_in
        g_mixed[branch, :, 0:N] = d_w
        g_mixed[branch, :, N : 2 * N] = d_r
        g_read[branch] = per_read
        g_write[branch] = per_write
        spread = head_rows()
        stride_e[branch] = split(strides[branch], spread)
        run = runs[branch]
        last = run[L - 1 : L] if branch == 0 else run[0:1]
        decay_e[branch] = split(jnp.exp(last - run), spread)

    def unpair(branch):
        ks = (2 * branch, 2 * branch + 1)
        for k in ks:
            for copy in e_s[k]:
                copy.wait_recv()
            row = k % 2
            for q in range(4):
                far[k, q] = factors[branch, q, row : row + 1, :] * e_in[k, q] + sums[core, k, q]
            far_s[k] = push(far.at[k], far_in.at[k], 54 + k, mate)
            states[core, k] = e_in[k]
        for k in ks:
            far_s[k].wait_recv()
            states[1 - core, k] = far_in[k]

    def joined(branch):
        way = (0, 1) if branch == 0 else (1, 0)

        def whole(direction):
            return jnp.concatenate(
                [states[direction, 2 * branch + h % 2, h // 2] for h in range(H)], axis=0
            )

        local = (
            g_x[branch], g_mixed[branch, :, 0:N], g_mixed[branch, :, N : 2 * N], g_read[branch],
            g_write[branch],
        )
        full_x, full_pre, g_writer, g_reader = full_grads(
            branch, x[branch], mixed[branch], zs[branch], strides[branch], runs[branch], rate[...],
            stride_e[branch], decay_e[branch], carried[branch], grown[branch], whole(way[0]),
            whole(way[1]), local,
        )
        d_x[branch] = full_x.astype(BF16)
        d_pre[branch] = full_pre.astype(BF16)
        for column, value in ((0, g_writer), (N, g_reader)):
            high = value.astype(BF16)
            d_mixed[branch, 0, :, column : column + N] = high
            d_mixed[branch, 1, :, column : column + N] = (value - high.astype(F32)).astype(BF16)

    def back(branch, weights, rows):
        dt_cols = weights[2][:, rows].astype(F32).T.astype(BF16)
        total = lax.dot_general(weights[0][rows, :], d_x[branch], NT, preferred_element_type=F32)
        for term in range(2):
            total = total + lax.dot_general(
                weights[1][rows, :], d_mixed[branch, term], NT, preferred_element_type=F32
            )
        return total + lax.dot_general(dt_cols, d_pre[branch], NT, preferred_element_type=F32)

    loads[0].wait()
    layer = embed(tokens[...], embedding[...], residual[...])
    for copy in loads[1:]:
        copy.wait()
    ups[...] = cotangent[...].astype(F32)
    front(0, layer)
    pl.semaphore_wait(barrier, 13)
    pair(0)
    for block in range(WIDTH // TILE):
        cols = slice(TILE * block, TILE * block + TILE)
        hot = permutation(pairing[:, cols], 0, TILE, 1)
        source[:, cols] = jnp.dot(layer, hot, preferred_element_type=F32).astype(BF16)
    front(1, source[...])
    pair(1)
    @pl.loop(0, WIDTH // TILE)
    def _(block):
        rows = pl.ds(pl.multiple_of(block * TILE, TILE), TILE)
        hot = permutation(pairing[...], block * TILE, TILE, 0)
        for weight, target in ((x_weight, x_paired), (bc_weight, bc_paired)):
            target[rows, :] = jnp.dot(hot, weight[...], preferred_element_type=F32).astype(BF16)
        dt_paired[:, rows] = lax.dot_general(
            dt_rows[...], hot, NT, preferred_element_type=F32
        ).astype(BF16)

    z_step(0)
    z_step(1)
    x_step(0)
    y_step(0)
    z_step(2)
    x_step(1)
    y_step(1)
    z_step(3)
    x_step(2)
    y_step(2)
    x_step(3)
    y_step(3)
    layer_t[...] = layer.astype(F32).T.astype(BF16)
    alone(0)
    alone(1)
    unpair(0)
    joined(0)
    rows_here = WIDTH // 4
    for block in range(4):
        rows = slice(rows_here * block, rows_here * block + rows_here)
        forward[rows, :] = back(0, (x_weight, bc_weight, dt_rows), rows)
    unpair(1)
    joined(1)

    def chunk(owner):
        rows = pl.ds(pl.multiple_of(owner * rows_here, rows_here), rows_here)
        total = forward[rows, :] + back(1, (x_paired, bc_paired, dt_paired), rows)
        weighed = jnp.sum(total * layer_t[rows, :].astype(F32), axis=0, keepdims=True)
        return total, weighed

    def handover(source_ref, target, sent, slot, index):
        return pltpu.make_async_remote_copy(
            src_ref=source_ref, dst_ref=target, send_sem=send_back.at[sent], recv_sem=recv_back.at[slot],
            device_id=(seq, index), device_id_type=MESH,
        )

    def give(*route):
        copy = handover(*route)
        copy.start()
        started.append(copy)
        return copy

    def arrived(index):
        pltpu.make_async_remote_copy(
            src_ref=part.at[0], dst_ref=got.at[index], send_sem=send_back.at[0],
            recv_sem=recv_back.at[index], device_id=(seq, 3 - head), device_id_type=MESH,
        ).wait_recv()

    edge = jnp.logical_or(head == 0, head == 3)
    near = jnp.where(head < 2, 1, 2)
    second = jnp.where(head == 0, 2, jnp.where(head == 1, 0, jnp.where(head == 2, 3, 1)))
    third = jnp.where(head == 0, 1, jnp.where(head == 1, 3, jnp.where(head == 2, 0, 2)))
    slot = jnp.where(edge, 0, 1)
    total, weighed = chunk(3 - head)
    part[0] = total
    route = [
        (part.at[0], got.at[slot], 0, slot, jnp.where(edge, near, 3 - head)),
        (part.at[1], got.at[2], 1, 2, second),
        (part.at[2], got.at[3], 2, 3, third),
    ]
    handover(*route[0]).start()
    total, share = chunk(second)
    weighed = weighed + share
    part[1] = total

    @pl.when(jnp.logical_not(edge))
    def _():
        handover(*route[1]).start()

    total, share = chunk(third)
    weighed = weighed + share
    part[2] = total
    total, share = chunk(head)
    weighed = weighed + share
    grad[...] = total
    sal_part[...] = jnp.broadcast_to(weighed, (8, L))
    sal_got[head] = sal_part[...]
    scan_sends = list(started)
    del started[:]
    shares = [
        give(sal_part, sal_got.at[head], 2 + d, 3 + d, h_peer[d - 1][1]) for d in (1, 2, 3)
    ]

    @pl.when(edge)
    def _():
        handover(*route[0]).wait_send()
        handover(*route[1]).start()
        handover(*route[2]).start()

    @pl.when(jnp.logical_not(edge))
    def _():
        arrived(0)
        part[2] = part[2] + got[0]
        handover(*route[2]).start()
        handover(*route[0]).wait_send()

    for copy in scan_sends:
        copy.wait_send()
    for copy in shares:
        copy.wait_recv()
    saliency[...] = (
        ((sal_got[0, 0:1] + sal_got[1, 0:1]) + sal_got[2, 0:1]) + sal_got[3, 0:1]
    ) / math.sqrt(WIDTH)

    @pl.when(jnp.logical_not(edge))
    def _():
        arrived(1)
        grad[...] = grad[...] + got[1]

    arrived(2)
    grad[...] = grad[...] + got[2]
    arrived(3)
    grad[...] = grad[...] + got[3]
    handover(*route[1]).wait_send()
    handover(*route[2]).wait_send()
    for copy in started:
        copy.wait_send()


VM = pl.BlockSpec(memory_space=pltpu.VMEM)
AT = pl.BlockSpec(memory_space=pl.ANY)


def final_kernel(grad, saliency, grad_out, saliency_out):
    grad_out[...] = grad[...]
    saliency_out[...] = saliency[...]


def shards(
    tokens, residual_in, pairing, embedding, x_weight, bc_weight, dt_weight, dt_bias, decay_rate,
    skip_gain, cotangent,
):
    tokens_row, pairing_row = tokens.reshape(1, L), pairing.reshape(1, WIDTH)
    bias, rate, skip = (value.reshape(1, H) for value in (dt_bias, decay_rate, skip_gain))
    shapes = [
        ((L, WIDTH), BF16), ((WIDTH, L), BF16), ((L, HP), F32), ((2, L, HP), F32),
        ((2, L, 2 * N), F32), ((2, L, H), F32), ((2, L, H), F32), ((2, L, H), F32),
        ((2, L, HP), F32), ((2, L, HP), F32), ((2, L, HP), BF16), ((2, L, HP), F32),
        ((2, L, HP), F32), ((2, L, 2 * N), F32), ((2, L, H), F32), ((2, L, H), F32),
        ((WIDTH, HP), BF16), ((WIDTH, 2 * N), BF16), ((H, WIDTH), BF16),
        ((2, 4, 4, 64, N), F32), ((2, 4, 8, N), F32), ((4, 4, 64, N), F32), ((2, 4, 8, N), F32),
        ((4, 4, 72, N), F32), ((4, 4, 72, N), F32), ((4, 4, 64, N), F32), ((4, 4, 72, N), F32),
        ((4, 4, 72, N), F32), ((4, 4, 64, N), F32), ((4, 4, 64, N), F32), ((4, 4, 64, N), F32),
        ((4, 4, 64, N), F32), ((2, 8, N), F32), ((2, 4, 8, N), F32), ((2, 4, 4, 64, N), F32),
        ((2, L, HP), BF16), ((2, 2, L, 2 * N), BF16), ((2, L, H), BF16), ((WIDTH, L), F32),
        ((3, WIDTH // 4, L), F32), ((4, WIDTH // 4, L), F32), ((8, L), F32), ((4, 8, L), F32),
    ]
    dma = pltpu.SemaphoreType.DMA
    grad, saliency = pl.pallas_call(
        kernel,
        out_shape=[
            jax.ShapeDtypeStruct((WIDTH // 4, L), F32), jax.ShapeDtypeStruct((1, L), F32),
        ],
        in_specs=[AT if index in (1, 4, 5, 10) else VM for index in range(11)],
        out_specs=[VM] * 2,
        scratch_shapes=[
            pltpu.VMEM((L, WIDTH), BF16), pltpu.VMEM((WIDTH, HP), BF16),
            pltpu.VMEM((WIDTH, 2 * N), BF16), pltpu.VMEM((L, HP), BF16), dma((4,)),
        ]
        + [pltpu.VMEM(*shape) for shape in shapes]
        + [dma((58,)), dma((58,)), dma((6,)), dma((7,))],
        compiler_params=pltpu.CompilerParams(
            collective_id=0, has_side_effects=True, vmem_limit_bytes=60 << 20
        ),
    )(
        tokens_row, residual_in, pairing_row, embedding, x_weight, bc_weight, dt_weight.T, bias, rate,
        skip, cotangent,
    )
    grad, saliency = pl.pallas_call(
        final_kernel,
        out_shape=[
            jax.ShapeDtypeStruct((WIDTH // 4, L), F32), jax.ShapeDtypeStruct((1, L), F32),
        ],
        in_specs=[VM] * 2,
        out_specs=[VM] * 2,
        compiler_params=pltpu.CompilerParams(vmem_limit_bytes=60 << 20),
    )(grad, saliency)
    return grad, saliency.reshape(L)


def solution(mesh):
    return jax.shard_map(
        shards,
        mesh=mesh,
        in_specs=(
            P("seq"), P("seq", None), P(), P(), P(None, "head"), P(), P(None, "head"), P("head"),
            P("head"), P("head"), P("seq", "head"),
        ),
        out_specs=(P("head", "seq"), P("seq")),
        check_vma=False,
    )
```
